512 devices in a mesh: delay: 32 (over z, x_hi), src: 8 (over x_lo, y), tgt: 2 (over core).
Axes of the slice: x: 4 (x_hi: 2, x_lo: 2; x = x_hi * 2 + x_lo), y: 4, z: 16, core: 2. Of those that a mesh axis runs over, the one named last changes fastest.
Arguments:
- blocks: bfloat16 [32, 8, 2, 32, 128, 128], P('delay', 'src', 'tgt'), may hold values from -0.0390625 to 0.0390625
- coords: int32 [32, 8, 2, 32, 2], P('delay', 'src', 'tgt'), may hold values from 0 to 31, as said below
- counts: int32 [32, 8, 2], P('delay', 'src', 'tgt'), may hold values from 16 to 32, as said below
- history: bfloat16 [32, 2, 4096, 128], P('delay', None, 'src'), may hold values from -6 to 6
- excitation: bfloat16 [2, 2, 4096, 128], P(None, 'tgt', 'src'), may hold values from -6 to 6
- inverse: bfloat16 [2, 32, 128, 128], P('tgt', 'src'), may hold values from -0.5 to 0.5
Outputs:
- currents: bfloat16 [2, 2, 4096, 128], P(None, 'tgt', 'src')
The draws below stay inside these ranges and needn't reach their ends.
Inputs may be any that keep to these rules, and one draw needn't show every extreme that they name: `counts`: at most 32 used slots in a tile; in every draw some tile has exactly 32. `coords`: within one tile the 32 slots name distinct (row block, column block) pairs, row blocks below 32 and column blocks below 8; slots at or past the tile's count are not used.
All inputs are finite; a program needn't handle non-finite values.
Results may differ from the reference program's by a relative error of at most 0.017.
Values may be sent and summed in bfloat16 or wider, within the bound.
A program may use at most 64 MiB of HBM per device.

```python
import jax
import jax.numpy as jnp
from jax import lax

E = 128
BLK = 128
N = 8192
CAP = 32
STEPS = 2
BINS = 32
N_SRC = 8
N_TGT = 2


def draw_counts(key, part):
    tile_count = BINS * N_SRC * N_TGT
    values = jax.random.randint(key, (tile_count,), CAP // 2, CAP + 1)
    chosen = jax.random.randint(jax.random.fold_in(key, 7), (), 0, tile_count)
    values = values.at[chosen].set(CAP)
    return values.reshape(BINS, N_SRC, N_TGT).astype(jnp.int32)


def draw_coords(key, part):
    row_count = N // (N_TGT * BLK)
    col_count = N // (N_SRC * BLK)
    places = row_count * col_count
    tile_count = BINS * N_SRC * N_TGT
    scores = jax.random.randint(key, (tile_count, places), 0, 1 << 16) * places
    scores = scores + jnp.arange(places, dtype=jnp.int32)[None, :]
    ranked = jnp.argsort(scores, axis=1)[:, :CAP].astype(jnp.int32)
    pairs = jnp.stack([ranked // col_count, ranked % col_count], axis=-1)
    return pairs.reshape(BINS, N_SRC, N_TGT, CAP, 2).astype(jnp.int32)


def block_scale(rng, dims, split, low, largest):
    def one(position, blocks):
        heights = jax.random.uniform(jax.random.fold_in(jax.random.fold_in(rng, 6), position), (blocks,), jnp.float32, low / len(split), largest / len(split))
        return jnp.repeat(jnp.exp(heights), dims[position] // blocks).reshape((-1,) + (1,) * (len(dims) - position - 1))

    factor_of = one(*split[0])
    for cut in split[1:]:
        factor_of = factor_of * one(*cut)
    return factor_of


def normal_values(stream_key, dims, width, most, cuts=(), held_as=jnp.bfloat16):
    array = width * jax.random.normal(stream_key, dims, jnp.float32)
    if cuts:
        array = array * block_scale(stream_key, dims, cuts, -0.22, 0.18)
    return jnp.clip(array, -most, most).astype(held_as)


def setup_inputs(seed: int = 0) -> dict:
    key_list = jax.random.split(jax.random.key(seed), 7)
    return {
        "blocks": normal_values(key_list[0], (BINS, N_SRC, N_TGT, CAP, BLK, BLK), (3 * CAP * N_SRC * BINS * BLK * BLK * N_TGT // (4 * N)) ** -0.5, 0.0390625, ((0, 32), (1, 8), (2, 2))),
        "coords": draw_coords(jax.random.fold_in(key_list[6], 71), 0),
        "counts": draw_counts(jax.random.fold_in(key_list[6], 71), 0),
        "history": normal_values(key_list[3], (BINS, N_TGT, N // N_TGT, E), 1.0, 6.0, ((0, 32), (2, 8))),
        "excitation": normal_values(key_list[4], (STEPS, N_TGT, N // N_TGT, E), 1.0, 6.0, ((1, 2), (2, 8))),
        "inverse": normal_values(key_list[5], (N_TGT, N // (N_TGT * BLK), BLK, BLK), BLK ** -0.5, 0.5, ((0, 2), (1, 8))),
    }


def tile_partial(slot_blocks, slot_places, slot_total, tile_cur):
    col_count = N // (N_SRC * BLK)
    row_count = N // (N_TGT * BLK)
    pieces = tile_cur.reshape(col_count, BLK, E)[slot_places[:, 1]]
    live_slots = (lax.iota(jnp.int32, CAP) < slot_total).astype(jnp.float32)
    products = jnp.einsum("cij,cjw->ciw", slot_blocks.astype(jnp.float32), pieces.astype(jnp.float32))
    products = products * live_slots[:, None, None]
    summed = jax.ops.segment_sum(products, slot_places[:, 0], num_segments=row_count)
    return summed.reshape(row_count * BLK, E)


def reference(blocks, coords, counts, history, excitation, inverse):
    owned_rows = N // (N_TGT * N_SRC)
    row_count = N // (N_TGT * BLK)
    results = []
    for moment in range(STEPS):
        if moment > 0:
            earlier = jnp.stack([results[moment - 1 - lag] for lag in range(moment)])
            lagged = jnp.concatenate([earlier, history[: BINS - moment]], axis=0)
        else:
            lagged = history

        def add_bin(bin_index, field_sum):
            tile_set = lagged[bin_index].reshape(N_TGT, N_SRC, owned_rows, E).transpose(1, 0, 2, 3)
            inner = jax.vmap(tile_partial, in_axes=(0, 0, 0, None))
            per_tile = jax.vmap(inner, in_axes=(0, 0, 0, 0))(blocks[bin_index], coords[bin_index], counts[bin_index], tile_set)
            rounded = lax.optimization_barrier(per_tile.astype(jnp.bfloat16)).astype(jnp.float32)
            return field_sum + jnp.sum(rounded, axis=0)

        field_sum = lax.fori_loop(0, BINS, add_bin, jnp.zeros((N_TGT, N // N_TGT, E), jnp.float32))
        drive_rows = (excitation[moment].astype(jnp.float32) - field_sum).astype(jnp.bfloat16)
        drive_rows = drive_rows.reshape(N_TGT, row_count, BLK, E)
        current = jnp.einsum("tbij,tbjw->tbiw", inverse.astype(jnp.float32), drive_rows.astype(jnp.float32))
        results.append(current.reshape(N_TGT, N // N_TGT, E).astype(jnp.bfloat16))
    return jnp.stack(results)
```

```python
import functools

import jax
import jax.numpy as jnp
from jax import lax
from jax.experimental import pallas as pl
from jax.experimental.pallas import tpu as pltpu
from jax.sharding import PartitionSpec as P

MESH = pl.DeviceIdType.MESH
F32 = jnp.float32
BF16 = jnp.bfloat16


def rcopy(src, dst, send, recv, device):
    return pltpu.make_async_remote_copy(
        src_ref=src, dst_ref=dst, send_sem=send, recv_sem=recv, device_id=device, device_id_type=MESH
    )


def drain(ref, sem):
    pltpu.make_async_copy(ref, ref, sem).wait()


def loop(count, body):
    def step(i, carry):
        body(i)
        return carry

    lax.fori_loop(0, count, step, 0)


def kernel(
    K, Y,
    idx, key, blocks, hist, exc, inv, out,
    bv, xv, ev, iv, pa, pb, ra, rb, qa, qb, sa, sb, zs, zr, dv, sl, kv, ad, us, ur, ov,
    ld, a1s, a1r, b1s, b1r, a2s, a2r, b2s, b2r, zss, zrs, gss, grs, uss, urs, hs, hr, cs, cr, os,
):
    k, s, h = lax.axis_index("delay"), lax.axis_index("src"), lax.axis_index("tgt")
    Z = K // 2
    S = 2 * Y
    zi = 128 // Z
    z, xh = k // 2, k % 2
    xl, y = s // Y, s % Y
    x = xh * 2 + xl
    e = s * 2 + h

    def at_x(other):
        return (z * 2 + other // 2, (other % 2) * Y + y, h)

    def at_y(other):
        return (k, xl * Y + other, h)

    loads = [
        pltpu.make_async_copy(blocks, bv.at[pl.ds(0, 32)], ld.at[0]),
        pltpu.make_async_copy(hist, xv.at[0], ld.at[1]),
        pltpu.make_async_copy(inv, iv, ld.at[2]),
    ]
    for step in range(2):
        for bb in range(2):
            loads.append(pltpu.make_async_copy(
                exc.at[step, 2 * xh + bb, pl.ds(z * zi, zi)], ev.at[step, bb], ld.at[3 + step * 2 + bb]))
    for copy in loads:
        copy.start()
    bv[32] = jnp.zeros((128, 128), BF16)

    barrier = pltpu.get_barrier_semaphore()
    loop(K - 1, lambda i: pl.semaphore_signal(
        barrier, inc=1, device_id=((k + 1 + i) % K, s, h), device_id_type=MESH))

    def greet(i):
        other = (e + 1 + i) % (2 * S)
        pl.semaphore_signal(barrier, inc=1, device_id=(k, other // 2, other % 2), device_id_type=MESH)

    loop(2 * S - 1, greet)
    pl.semaphore_signal(barrier, inc=1, device_id=at_x(3 - x), device_id_type=MESH)
    for copy in loads:
        copy.wait()
    pl.semaphore_wait(barrier, (K - 1) + (2 * S - 1) + 1)

    @pl.when(k == 0)
    def _():
        def give(i):
            other = 1 + i
            rcopy(blocks.at[:, pl.ds(other * zi, zi)], sl.at[h], cs.at[0], cr.at[0], (other * 2, s, h)).start()
            rcopy(key, kv.at[h], cs.at[1], cr.at[1], (other * 2, s, h)).start()

        loop(Z - 1, give)
        mine = pltpu.make_async_copy(blocks.at[:, pl.ds(0, zi)], sl.at[h], cr.at[0])
        mine.start()
        also = pltpu.make_async_copy(key, kv.at[h], cr.at[1])
        also.start()

    def row_block(xx, yy, bb):
        return 4 * ((xx % 2) * Y + yy) + 2 * (xx // 2) + bb

    def block_sum(step, r):
        total = None
        for jp in range(4):
            left = bv[idx[r * 8 + 2 * jp]]
            right = bv[idx[r * 8 + 2 * jp + 1]]
            term = jnp.dot(jnp.concatenate([left, right], axis=1), xv[step, jp], preferred_element_type=F32)
            total = term if total is None else total + term
        return total.astype(BF16)

    def first_stage(step, live):
        for i in range(4):
            dx = (i + 2) % 4
            xx = (x + dx) % 4

            def fill_a(u):
                if live is None:
                    pa[step, xx, u] = block_sum(step, row_block(xx, u, 0))
                else:
                    @pl.when(live)
                    def _():
                        pa[step, xx, u] = block_sum(step, row_block(xx, u, 0))

                    @pl.when(jnp.logical_not(live))
                    def _():
                        pa[step, xx, u] = jnp.zeros((128, 128), BF16)

            loop(Y, fill_a)
            if dx:
                rcopy(pa.at[step, xx], ra.at[step, dx - 1], a1s.at[step, dx - 1], a1r.at[step, dx - 1], at_x(xx)).start()
            if i < Y:
                dy = (i + Y // 2) % Y
                yy = (y + dy) % Y

                def fill_b(u):
                    if live is None:
                        pb[step, yy, u] = block_sum(step, row_block(u, yy, 1))
                    else:
                        @pl.when(live)
                        def _():
                            pb[step, yy, u] = block_sum(step, row_block(u, yy, 1))

                        @pl.when(jnp.logical_not(live))
                        def _():
                            pb[step, yy, u] = jnp.zeros((128, 128), BF16)

                loop(4, fill_b)
                if dy:
                    rcopy(pb.at[step, yy], rb.at[step, dy - 1], b1s.at[step, dy - 1], b1r.at[step, dy - 1], at_y(yy)).start()

    def second_stage(step):
        for d in range(3):
            drain(ra.at[step, d], a1r.at[step, d])
        total = pa[step, x].astype(F32)
        for d in range(3):
            total += ra[step, d].astype(F32)
        qa[step] = total.astype(BF16)
        for dy in [Y // 2] + [d for d in range(1, Y) if d != Y // 2]:
            yy = (y + dy) % Y
            rcopy(qa.at[step, yy], sa.at[step, dy - 1], a2s.at[step, dy - 1], a2r.at[step, dy - 1], at_y(yy)).start()
        for d in range(Y - 1):
            drain(rb.at[step, d], b1r.at[step, d])
        total = pb[step, y].astype(F32)
        for d in range(Y - 1):
            total += rb[step, d].astype(F32)
        qb[step] = total.astype(BF16)
        for dx in (2, 1, 3):
            xx = (x + dx) % 4
            rcopy(qb.at[step, xx], sb.at[step, dx - 1], b2s.at[step, dx - 1], b2r.at[step, dx - 1], at_x(xx)).start()

    def far_first(i):
        return Z // 2 + (1 - 2 * (i % 2)) * ((i + 1) // 2)

    def third_stage(step):
        for d in range(Y - 1):
            drain(sa.at[step, d], a2r.at[step, d])
        first = qa[step, y].astype(F32)
        for d in range(Y - 1):
            first += sa[step, d].astype(F32)
        for d in range(3):
            drain(sb.at[step, d], b2r.at[step, d])
        second = qb[step, x].astype(F32)
        for d in range(3):
            second += sb[step, d].astype(F32)
        both = jnp.concatenate([first.reshape(Z, zi, 128), second.reshape(Z, zi, 128)], axis=1)
        zs[step] = both.astype(BF16)

        def give(i):
            other = (z + far_first(i)) % Z
            rcopy(zs.at[step, other], zr.at[step, z], zss.at[step], zrs.at[step], (other * 2 + xh, s, h)).start()

        loop(Z - 1, give)

    def field(step):
        drain(zr.at[step, pl.ds(0, Z - 1)], zrs.at[step])
        zr[step, z] = zs[step, z]
        return jnp.sum(zr[step].astype(F32), axis=0)

    def gather(step, total):
        incident = jnp.concatenate([ev[step, 0].astype(F32), ev[step, 1].astype(F32)], axis=0)
        dv[step, xh * Z + z] = (incident - total).astype(BF16)
        here = dv.at[step, xh * Z + z]

        def give(i):
            other = (z + far_first(i)) % Z
            rcopy(here, here, gss.at[step], grs.at[step], (other * 2 + (1 - xh), s, h)).start()
            rcopy(here, here, gss.at[step], grs.at[step], (other * 2 + xh, s, h)).start()

        loop(Z - 1, give)
        rcopy(here, here, gss.at[step], grs.at[step], (z * 2 + (1 - xh), s, h)).start()

    def currents(step):
        drain(dv.at[step, pl.ds(0, K - 1)], grs.at[step])
        for half in range(2):
            chunk = dv[step, half * Z:(half + 1) * Z].astype(F32)
            for bb in range(2):
                drive = chunk[:, bb * zi:(bb + 1) * zi, :].reshape(128, 128).astype(BF16)
                b = 2 * half + bb
                ov[step, b] = jnp.dot(iv[b], drive, preferred_element_type=F32).astype(BF16)
        pltpu.make_async_copy(ov.at[step], out.at[step], os.at[step]).start()

    first_stage(0, None)

    mine = pl.ds(2 * h, 2)

    @pl.when(k < K - 1)
    def _():
        rcopy(hist.at[mine], xv.at[1, mine], hs.at[0], hr.at[0], (k + 1, s, h)).start()

    second_stage(0)

    @pl.when(xh == 0)
    def _():
        drain(sl.at[h], cr.at[0])
        drain(kv.at[h], cr.at[1])
        rcopy(sl.at[h], sl.at[h], cs.at[2], cr.at[0], (k + 1, s, h)).start()
        rcopy(kv.at[h], kv.at[h], cs.at[3], cr.at[1], (k + 1, s, h)).start()
        rcopy(sl.at[h], sl.at[h], cs.at[4], cr.at[2], (k, s, 1 - h)).start()
        rcopy(kv.at[h], kv.at[h], cs.at[5], cr.at[3], (k, s, 1 - h)).start()

    @pl.when(k > 0)
    def _():
        drain(xv.at[1, mine], hr.at[0])
        rcopy(xv.at[1, mine], xv.at[1, mine], hs.at[1], hr.at[1], (k, s, 1 - h)).start()

    third_stage(0)

    @pl.when(k > 0)
    def _():
        drain(xv.at[1, pl.ds(2 - 2 * h, 2)], hr.at[1])

    first_stage(1, k > 0)
    gather(0, field(0))

    @pl.when(xh == 1)
    def _():
        drain(sl.at[h], cr.at[0])
        drain(kv.at[h], cr.at[1])
        rcopy(sl.at[h], sl.at[h], cs.at[4], cr.at[2], (k, s, 1 - h)).start()
        rcopy(kv.at[h], kv.at[h], cs.at[5], cr.at[3], (k, s, 1 - h)).start()

    second_stage(1)

    drain(sl.at[1 - h], cr.at[2])
    drain(kv.at[1 - h], cr.at[3])
    rows, wide = S * 2 * zi, 32 * zi
    m = lax.broadcasted_iota(jnp.int32, (rows, wide), 0)
    n = lax.broadcasted_iota(jnp.int32, (rows, wide), 1)
    q = m // zi
    place = (4 * (q // 2) + 2 * xh + q % 2) * 8 + 4 * h
    same = (m % zi) == (n % zi)
    for half in range(2):
        slots = sl[half].astype(F32).reshape(wide, 128).astype(BF16)
        where = jnp.broadcast_to(kv[half, 0:1, :], (rows, wide))
        for jj in range(4):
            pick = jnp.where(same & (where == place + jj), 1.0, 0.0).astype(BF16)
            ad[half, :, jj * 128:(jj + 1) * 128] = jnp.dot(pick, slots, preferred_element_type=F32).astype(BF16)

    third_stage(1)
    currents(0)

    newest = ov[0].reshape(512, 128)
    for half in range(2):
        made = jnp.dot(ad[half], newest, preferred_element_type=F32).astype(BF16)
        for other in range(S):
            us[other * 2 + half] = made[other * 2 * zi:(other + 1) * 2 * zi]

    def share(i):
        other = (e + 1 + i) % (2 * S)
        rcopy(us.at[other], ur.at[e], uss.at[0], urs.at[0], (k, other // 2, other % 2)).start()

    loop(2 * S - 1, share)
    rest = field(1)
    drain(ur.at[pl.ds(0, 2 * S - 1)], urs.at[0])
    ur[e] = us[e]
    gather(1, rest + jnp.sum(ur[...].astype(F32), axis=0))
    currents(1)

    for step in range(2):
        for d in range(3):
            drain(pa.at[step, 0], a1s.at[step, d])
            drain(qb.at[step, 0], b2s.at[step, d])
        for d in range(Y - 1):
            drain(pb.at[step, 0], b1s.at[step, d])
            drain(qa.at[step, 0], a2s.at[step, d])
        drain(zs.at[step, pl.ds(0, Z - 1)], zss.at[step])
        drain(dv.at[step, pl.ds(0, K - 1)], gss.at[step])
    drain(us.at[pl.ds(0, 2 * S - 1)], uss.at[0])

    @pl.when(k < K - 1)
    def _():
        drain(xv.at[1, mine], hs.at[0])

    @pl.when(k > 0)
    def _():
        drain(xv.at[1, mine], hs.at[1])

    @pl.when(k == 0)
    def _():
        drain(bv.at[pl.ds(0, 32 - 32 // Z)], cs.at[0])
        drain(dv.at[0, pl.ds(0, 2 * Z - 2)], cs.at[1])

    @pl.when(xh == 0)
    def _():
        drain(sl.at[h], cs.at[2])
        drain(kv.at[h], cs.at[3])

    drain(sl.at[h], cs.at[4])
    drain(kv.at[h], cs.at[5])
    for step in range(2):
        pltpu.make_async_copy(ov.at[step], out.at[step], os.at[step]).wait()


def shards(K, S, blocks, coords, counts, history, excitation, inverse):
    Y, Z = S // 2, K // 2
    zi = 128 // Z
    slots = lax.iota(jnp.int32, 32)
    places = coords[0, 0, 0]
    key = jnp.where(slots < counts[0, 0, 0], places[:, 0] * 8 + places[:, 1], -1)
    cells = lax.iota(jnp.int32, 4 * S * 8)
    idx = jnp.min(jnp.where(key[:, None] == cells[None, :], slots[:, None], 32), axis=0)
    wide = jnp.broadcast_to(key[None, :, None], (8, 32, zi)).reshape(8, 32 * zi)
    dma = pltpu.SemaphoreType.DMA
    v = pltpu.VMEM
    scratch = [
        v((33, 128, 128), BF16), v((2, 4, 256, 128), BF16), v((2, 2, zi, 128), BF16), v((4, 128, 128), BF16),
        v((2, 4, Y, 128, 128), BF16), v((2, Y, 4, 128, 128), BF16),
        v((2, 3, Y, 128, 128), BF16), v((2, Y - 1, 4, 128, 128), BF16),
        v((2, Y, 128, 128), BF16), v((2, 4, 128, 128), BF16),
        v((2, Y - 1, 128, 128), BF16), v((2, 3, 128, 128), BF16),
        v((2, Z, 2 * zi, 128), BF16), v((2, Z, 2 * zi, 128), BF16), v((2, K, 2 * zi, 128), BF16),
        v((2, 32, zi, 128), BF16), v((2, 8, 32 * zi), jnp.int32), v((2, S * 2 * zi, 512), BF16),
        v((2 * S, 2 * zi, 128), BF16), v((2 * S, 2 * zi, 128), BF16), v((2, 4, 128, 128), BF16),
        dma((7,)), dma((2, 3)), dma((2, 3)), dma((2, Y - 1)), dma((2, Y - 1)),
        dma((2, Y - 1)), dma((2, Y - 1)), dma((2, 3)), dma((2, 3)),
        dma((2,)), dma((2,)), dma((2,)), dma((2,)), dma((1,)), dma((1,)), dma((2,)), dma((2,)), dma((6,)), dma((4,)), dma((2,)),
    ]
    any_ = pl.BlockSpec(memory_space=pl.ANY)
    made = pl.pallas_call(
        functools.partial(kernel, K, Y),
        out_shape=jax.ShapeDtypeStruct((2, 4, 128, 128), BF16),
        in_specs=[pl.BlockSpec(memory_space=pltpu.SMEM)] + [any_] * 5,
        out_specs=any_,
        scratch_shapes=scratch,
        compiler_params=pltpu.CompilerParams(
            collective_id=0, has_side_effects=True, vmem_limit_bytes=40 * 1024 * 1024),
        name="march",
    )(
        idx, wide, blocks[0, 0, 0], history[0].reshape(4, 256, 128),
        excitation[:, 0].reshape(2, 4, 128, 128), inverse[0],
    )
    return made.reshape(2, 1, 512, 128)


def solution(mesh):
    placed = (
        P("delay", "src", "tgt", None, None, None),
        P("delay", "src", "tgt", None, None),
        P("delay", "src", "tgt"),
        P("delay", None, "src", None),
        P(None, "tgt", "src", None),
        P("tgt", "src", None, None),
    )
    return jax.shard_map(
        functools.partial(shards, mesh.shape["delay"], mesh.shape["src"]),
        mesh=mesh, in_specs=placed, out_specs=P(None, "tgt", "src", None), check_vma=False,
    )
```

```python
import functools

import jax
import jax.numpy as jnp
from jax import lax
from jax.experimental import pallas as pl
from jax.experimental.pallas import tpu as pltpu
from jax.sharding import PartitionSpec as P

MESH = pl.DeviceIdType.MESH
F32 = jnp.float32
BF16 = jnp.bfloat16


def rcopy(src, dst, send, recv, device):
    return pltpu.make_async_remote_copy(
        src_ref=src, dst_ref=dst, send_sem=send, recv_sem=recv, device_id=device, device_id_type=MESH
    )


def drain(ref, sem):
    pltpu.make_async_copy(ref, ref, sem).wait()


def wrap(value, size):
    return lax.rem(value, size)


def loop(count, body):
    def step(i, carry):
        body(i)
        return carry

    lax.fori_loop(0, count, step, 0)


def kernel(
    K, Y,
    tab, key, blocks, hist, exc, inv, out,
    bv, x0, x1, ev, iv, acc, dr, pa, pb, ra, rb, qa, qb, sa, sb, zs, zr, dv, sl, kv, ad, us, ur, ov,
    ld, a1s, a1r, b1s, b1r, a2s, a2r, b2s, b2r, zss, zrs, gss, grs, uss, urs, hs, hr, cs, cr, os,
):
    k, s, h = lax.axis_index("delay"), lax.axis_index("src"), lax.axis_index("tgt")
    Z = K // 2
    S = 2 * Y
    zi = 128 // Z
    z, xh = lax.div(k, 2), lax.rem(k, 2)
    xl, y = lax.div(s, Y), lax.rem(s, Y)
    x = xh * 2 + xl
    e = s * 2 + h

    def at_x(other):
        return (z * 2 + lax.div(other, 2), lax.rem(other, 2) * Y + y, h)

    def at_y(other):
        return (k, xl * Y + other, h)

    loads = [
        pltpu.make_async_copy(blocks, bv, ld.at[0]),
        pltpu.make_async_copy(hist, x0, ld.at[1]),
        pltpu.make_async_copy(inv, iv, ld.at[2]),
    ]
    for step in range(2):
        for bb in range(2):
            loads.append(pltpu.make_async_copy(
                exc.at[step, 2 * xh + bb, pl.ds(z * zi, zi)], ev.at[step, bb], ld.at[3 + step * 2 + bb]))
    for copy in loads:
        copy.start()

    barrier = pltpu.get_barrier_semaphore()

    def greet(device):
        pl.semaphore_signal(barrier, inc=1, device_id=device, device_id_type=MESH)

    for d in range(1, K):
        greet((wrap(k + d, K), s, h))
    for d in range(1, 2 * S):
        other = wrap(e + d, 2 * S)
        greet((k, lax.div(other, 2), lax.rem(other, 2)))
    greet(at_x(3 - x))

    acc[32] = jnp.zeros((128, 128), F32)

    def products(tile):
        def body(g):
            total = acc[wrap(4 * g + 32, 33)]
            for c in range(4):
                c = 4 * g + c
                made = jnp.dot(bv[tab[c]], tile[tab[32 + c]], preferred_element_type=F32)
                total = made + total * tab[64 + c].astype(F32)
                acc[c] = total

        loop(8, body)

    loads[0].wait()
    loads[1].wait()
    products(x0)
    for copy in loads[2:]:
        copy.wait()
    pl.semaphore_wait(barrier, (K - 1) + (2 * S - 1) + 1)

    @pl.when(k == 0)
    def _():
        def give(i):
            other = 1 + i
            rcopy(blocks.at[:, pl.ds(other * zi, zi)], sl.at[h], cs.at[0], cr.at[0], (other * 2, s, h)).start()
            rcopy(key, kv.at[h], cs.at[1], cr.at[1], (other * 2, s, h)).start()

        loop(Z - 1, give)
        mine = pltpu.make_async_copy(blocks.at[:, pl.ds(0, zi)], sl.at[h], cr.at[0])
        mine.start()
        also = pltpu.make_async_copy(key, kv.at[h], cr.at[1])
        also.start()

    def row_block(xx, yy, bb):
        return 4 * (lax.rem(xx, 2) * Y + yy) + 2 * lax.div(xx, 2) + bb

    def first_stage(step):
        for i in range(4):
            dx = (i + 2) % 4
            xx = wrap(x + dx, 4)

            def fill_a(u):
                pa[step, xx, u] = acc[tab[96 + row_block(xx, u, 0)]].astype(BF16)

            loop(Y, fill_a)
            if dx:
                rcopy(pa.at[step, xx], ra.at[step, dx - 1], a1s.at[step, dx - 1], a1r.at[step, dx - 1], at_x(xx)).start()
            if i < Y:
                dy = (i + Y // 2) % Y
                yy = wrap(y + dy, Y)

                def fill_b(u):
                    pb[step, yy, u] = acc[tab[96 + row_block(u, yy, 1)]].astype(BF16)

                loop(4, fill_b)
                if dy:
                    rcopy(pb.at[step, yy], rb.at[step, dy - 1], b1s.at[step, dy - 1], b1r.at[step, dy - 1], at_y(yy)).start()

    def second_stage(step):
        for d in range(3):
            drain(ra.at[step, d], a1r.at[step, d])
        total = pa[step, x].astype(F32)
        for d in range(3):
            total += ra[step, d].astype(F32)
        qa[step] = total.astype(BF16)
        for dy in [Y // 2] + [d for d in range(1, Y) if d != Y // 2]:
            yy = wrap(y + dy, Y)
            rcopy(qa.at[step, yy], sa.at[step, dy - 1], a2s.at[step, dy - 1], a2r.at[step, dy - 1], at_y(yy)).start()
        for d in range(Y - 1):
            drain(rb.at[step, d], b1r.at[step, d])
        total = pb[step, y].astype(F32)
        for d in range(Y - 1):
            total += rb[step, d].astype(F32)
        qb[step] = total.astype(BF16)
        for dx in (2, 1, 3):
            xx = wrap(x + dx, 4)
            rcopy(qb.at[step, xx], sb.at[step, dx - 1], b2s.at[step, dx - 1], b2r.at[step, dx - 1], at_x(xx)).start()

    def far_first(i):
        return Z // 2 + (1 - 2 * lax.rem(i, 2)) * lax.div(i + 1, 2)

    def third_stage(step):
        for d in range(Y - 1):
            drain(sa.at[step, d], a2r.at[step, d])
        first = qa[step, y].astype(F32)
        for d in range(Y - 1):
            first += sa[step, d].astype(F32)
        for d in range(3):
            drain(sb.at[step, d], b2r.at[step, d])
        second = qb[step, x].astype(F32)
        for d in range(3):
            second += sb[step, d].astype(F32)
        both = jnp.concatenate([first.reshape(Z, zi, 128), second.reshape(Z, zi, 128)], axis=1)
        zs[step] = both.astype(BF16)

        def give(i):
            other = wrap(z + far_first(i), Z)
            rcopy(zs.at[step, other], zr.at[step, z], zss.at[step], zrs.at[step], (other * 2 + xh, s, h)).start()

        loop(Z - 1, give)

    def field(step):
        drain(zr.at[step, pl.ds(0, Z - 1)], zrs.at[step])
        zr[step, z] = zs[step, z]
        return jnp.sum(zr[step].astype(F32), axis=0)

    def gather(step, total):
        incident = jnp.concatenate([ev[step, 0].astype(F32), ev[step, 1].astype(F32)], axis=0)
        dv[step, xh * Z + z] = (incident - total).astype(BF16)
        here = dv.at[step, xh * Z + z]

        if step == 0:
            def give(i):
                other = wrap(z + far_first(i), Z)
                for half in (1 - xh, xh):
                    rcopy(here, here, gss.at[step], grs.at[step], (other * 2 + half, s, h)).start()

            loop(Z - 1, give)
            rcopy(here, here, gss.at[step], grs.at[step], (z * 2 + (1 - xh), s, h)).start()
        else:
            rcopy(here, here, gss.at[step], grs.at[step], (z * 2 + (1 - xh), s, h)).start()

            def hand(i):
                other = i + (z <= i).astype(jnp.int32)
                for half in (1 - xh, xh):
                    rcopy(here, here, gss.at[step], grs.at[step], (other * 2 + half, s, h)).start()

            loop(Z - 1, hand)

    def driven(step):
        drain(dv.at[step, pl.ds(0, K - 1)], grs.at[step])
        for half in range(2):
            chunk = dv[step, half * Z:(half + 1) * Z].astype(F32)
            for bb in range(2):
                dr[step, 2 * half + bb] = chunk[:, bb * zi:(bb + 1) * zi, :].reshape(128, 128).astype(BF16)
        pltpu.make_async_copy(dr.at[step], out.at[step], os.at[step]).start()

    first_stage(0)

    mine = pl.ds(4 * h, 4)

    @pl.when(k < K - 1)
    def _():
        rcopy(hist.at[mine], x1.at[mine], hs.at[0], hr.at[0], (k + 1, s, h)).start()

    second_stage(0)

    @pl.when(xh == 0)
    def _():
        drain(sl.at[h], cr.at[0])
        drain(kv.at[h], cr.at[1])
        rcopy(sl.at[h], sl.at[h], cs.at[2], cr.at[0], (k + 1, s, h)).start()
        rcopy(kv.at[h], kv.at[h], cs.at[3], cr.at[1], (k + 1, s, h)).start()
        rcopy(sl.at[h], sl.at[h], cs.at[4], cr.at[2], (k, s, 1 - h)).start()
        rcopy(kv.at[h], kv.at[h], cs.at[5], cr.at[3], (k, s, 1 - h)).start()

    @pl.when(k > 0)
    def _():
        drain(x1.at[mine], hr.at[0])
        rcopy(x1.at[mine], x1.at[mine], hs.at[1], hr.at[1], (k, s, 1 - h)).start()

    third_stage(0)

    @pl.when(k > 0)
    def _():
        drain(x1.at[pl.ds(4 - 4 * h, 4)], hr.at[1])

    @pl.when(k > 0)
    def _():
        products(x1)

    @pl.when(k == 0)
    def _():
        def clear(c):
            acc[c] = jnp.zeros((128, 128), F32)

        loop(32, clear)

    first_stage(1)
    gather(0, field(0))

    @pl.when(xh == 1)
    def _():
        drain(sl.at[h], cr.at[0])
        drain(kv.at[h], cr.at[1])
        rcopy(sl.at[h], sl.at[h], cs.at[4], cr.at[2], (k, s, 1 - h)).start()
        rcopy(kv.at[h], kv.at[h], cs.at[5], cr.at[3], (k, s, 1 - h)).start()

    second_stage(1)

    drain(sl.at[1 - h], cr.at[2])
    drain(kv.at[1 - h], cr.at[3])
    rows, wide = S * 2 * zi, 32 * zi
    m = lax.broadcasted_iota(jnp.int32, (rows, wide), 0)
    n = lax.broadcasted_iota(jnp.int32, (rows, wide), 1)
    q = m // zi
    place = (4 * (q // 2) + 2 * xh + q % 2) * 8 + 4 * h
    same = (m % zi) == (n % zi)
    for half in range(2):
        slots = sl[half].astype(F32).reshape(wide, 128).astype(BF16)
        where = jnp.broadcast_to(kv[half, 0:1, :], (rows, wide))
        for jj in range(4):
            pick = jnp.where(same & (where == place + jj), 1.0, 0.0).astype(BF16)
            ad[half, :, jj * 128:(jj + 1) * 128] = jnp.dot(pick, slots, preferred_element_type=F32).astype(BF16)

    third_stage(1)
    driven(0)
    for b in range(4):
        ov[b * 128:(b + 1) * 128] = jnp.dot(iv[b], dr[0, b], preferred_element_type=F32).astype(BF16)
    newest = ov[...]
    for half in range(2):
        made = jnp.dot(ad[half], newest, preferred_element_type=F32).astype(BF16)
        for other in range(S):
            us[other * 2 + half] = made[other * 2 * zi:(other + 1) * 2 * zi]

    for d in list(range(S, 2 * S)) + list(range(1, S)):
        other = wrap(e + d, 2 * S)
        rcopy(us.at[other], ur.at[e], uss.at[0], urs.at[0], (k, lax.div(other, 2), lax.rem(other, 2))).start()

    rest = field(1)
    drain(ur.at[pl.ds(0, 2 * S - 1)], urs.at[0])
    ur[e] = us[e]
    gather(1, rest + jnp.sum(ur[...].astype(F32), axis=0))
    driven(1)

    for step in range(2):
        for d in range(3):
            drain(pa.at[step, 0], a1s.at[step, d])
            drain(qb.at[step, 0], b2s.at[step, d])
        for d in range(Y - 1):
            drain(pb.at[step, 0], b1s.at[step, d])
            drain(qa.at[step, 0], a2s.at[step, d])
        drain(zs.at[step, pl.ds(0, Z - 1)], zss.at[step])
        drain(dv.at[step, pl.ds(0, K - 1)], gss.at[step])
    drain(us.at[pl.ds(0, 2 * S - 1)], uss.at[0])

    @pl.when(k < K - 1)
    def _():
        drain(x1.at[mine], hs.at[0])

    @pl.when(k > 0)
    def _():
        drain(x1.at[mine], hs.at[1])

    @pl.when(k == 0)
    def _():
        drain(bv.at[pl.ds(0, 32 - 32 // Z)], cs.at[0])
        drain(dv.at[0, pl.ds(0, 2 * Z - 2)], cs.at[1])

    @pl.when(xh == 0)
    def _():
        drain(sl.at[h], cs.at[2])
        drain(kv.at[h], cs.at[3])

    drain(sl.at[h], cs.at[4])
    drain(kv.at[h], cs.at[5])
    for step in range(2):
        pltpu.make_async_copy(dr.at[step], out.at[step], os.at[step]).wait()


def shards(K, S, blocks, coords, counts, history, excitation, inverse):
    Y, Z = S // 2, K // 2
    zi = 128 // Z
    slots = lax.iota(jnp.int32, 32)
    places = coords[0, 0, 0]
    key = jnp.where(slots < counts[0, 0, 0], places[:, 0] * 8 + places[:, 1], 1 << 20)
    ahead = (key[None, :] < key[:, None]) | ((key[None, :] == key[:, None]) & (slots[None, :] < slots[:, None]))
    rank = jnp.sum(ahead.astype(jnp.int32), axis=1)
    chosen = rank[None, :] == slots[:, None]
    order = jnp.sum(jnp.where(chosen, slots[None, :], 0), axis=1)
    placed = jnp.sum(jnp.where(chosen, key[None, :], 0), axis=1)
    row = placed // 8
    before = jnp.sum(jnp.where(rank[None, :] == slots[:, None] - 1, key[None, :] // 8, 0), axis=1)
    keep = ((slots > 0) & (row == before)).astype(jnp.int32)
    last = jnp.max(jnp.where(key[None, :] // 8 == lax.iota(jnp.int32, 4 * S)[:, None], rank[None, :], -1), axis=1)
    last = jnp.where(last < 0, 32, last)
    tab = jnp.concatenate([order, placed % 8, keep, last])
    wide = jnp.broadcast_to(key[None, :, None], (8, 32, zi)).reshape(8, 32 * zi)
    dma = pltpu.SemaphoreType.DMA
    v = pltpu.VMEM
    scratch = [
        v((32, 128, 128), BF16), v((8, 128, 128), BF16), v((8, 128, 128), BF16), v((2, 2, zi, 128), BF16), v((4, 128, 128), BF16),
        v((33, 128, 128), F32), v((2, 4, 128, 128), BF16),
        v((2, 4, Y, 128, 128), BF16), v((2, Y, 4, 128, 128), BF16),
        v((2, 3, Y, 128, 128), BF16), v((2, Y - 1, 4, 128, 128), BF16),
        v((2, Y, 128, 128), BF16), v((2, 4, 128, 128), BF16),
        v((2, Y - 1, 128, 128), BF16), v((2, 3, 128, 128), BF16),
        v((2, Z, 2 * zi, 128), BF16), v((2, Z, 2 * zi, 128), BF16), v((2, K, 2 * zi, 128), BF16),
        v((2, 32, zi, 128), BF16), v((2, 8, 32 * zi), jnp.int32), v((2, S * 2 * zi, 512), BF16),
        v((2 * S, 2 * zi, 128), BF16), v((2 * S, 2 * zi, 128), BF16), v((512, 128), BF16),
        dma((7,)), dma((2, 3)), dma((2, 3)), dma((2, Y - 1)), dma((2, Y - 1)),
        dma((2, Y - 1)), dma((2, Y - 1)), dma((2, 3)), dma((2, 3)),
        dma((2,)), dma((2,)), dma((2,)), dma((2,)), dma((1,)), dma((1,)), dma((2,)), dma((2,)), dma((6,)), dma((4,)), dma((2,)),
    ]
    hbm = pl.BlockSpec(memory_space=pltpu.HBM)
    made = pl.pallas_call(
        functools.partial(kernel, K, Y),
        out_shape=jax.ShapeDtypeStruct((2, 4, 128, 128), BF16),
        in_specs=[pl.BlockSpec(memory_space=pltpu.SMEM)] + [hbm] * 5,
        out_specs=pl.BlockSpec(memory_space=pl.ANY),
        scratch_shapes=scratch,
        compiler_params=pltpu.CompilerParams(
            collective_id=0, has_side_effects=True, vmem_limit_bytes=67043328),
        name="march",
    )(
        tab, wide, blocks[0, 0, 0], history[0].reshape(8, 128, 128),
        excitation[:, 0].reshape(2, 4, 128, 128), inverse[0],
    )
    both = jnp.broadcast_to(inverse[0][None], made.shape)
    currents = jnp.einsum("nbij,nbjw->nbiw", both, made, preferred_element_type=F32)
    return currents.astype(BF16).reshape(2, 1, 512, 128)


def solution(mesh):
    placed = (
        P("delay", "src", "tgt", None, None, None),
        P("delay", "src", "tgt", None, None),
        P("delay", "src", "tgt"),
        P("delay", None, "src", None),
        P(None, "tgt", "src", None),
        P("tgt", "src", None, None),
    )
    return jax.shard_map(
        functools.partial(shards, mesh.shape["delay"], mesh.shape["src"]),
        mesh=mesh, in_specs=placed, out_specs=P(None, "tgt", "src", None), check_vma=False,
    )
```

```python
import functools

import jax
import jax.numpy as jnp
from jax import lax
from jax.experimental import pallas as pl
from jax.experimental.pallas import tpu as pltpu
from jax.sharding import PartitionSpec as P

MESH = pl.DeviceIdType.MESH
F32 = jnp.float32
BF16 = jnp.bfloat16


def rcopy(src, dst, send, recv, device):
    return pltpu.make_async_remote_copy(
        src_ref=src, dst_ref=dst, send_sem=send, recv_sem=recv, device_id=device, device_id_type=MESH
    )


def drain(ref, sem):
    pltpu.make_async_copy(ref, ref, sem).wait()


def wrap(value, size):
    return lax.rem(value, size)


def loop(count, body):
    def step(i, carry):
        body(i)
        return carry

    lax.fori_loop(0, count, step, 0)


def kernel(
    K, Y,
    tab, key, blocks, hist, exc, inv, out,
    bv, pk, x0, x1, ev, iv, acc, dr, pa, pb, ra, rb, qa, qb, sa, sb, zs, zr, dv, sl, kv, ad, us, ur, ov,
    ld, a1s, a1r, b1s, b1r, a2s, a2r, b2s, b2r, zss, zrs, gss, grs, uss, urs, hs, hr, cs, cr, os,
):
    k, s, h = lax.axis_index("delay"), lax.axis_index("src"), lax.axis_index("tgt")
    Z = K // 2
    S = 2 * Y
    zi = 128 // Z
    z, xh = lax.div(k, 2), lax.rem(k, 2)
    xl, y = lax.div(s, Y), lax.rem(s, Y)
    x = xh * 2 + xl
    e = s * 2 + h

    def at_x(other):
        return (z * 2 + lax.div(other, 2), lax.rem(other, 2) * Y + y, h)

    def at_y(other):
        return (k, xl * Y + other, h)

    loads = [
        pltpu.make_async_copy(blocks, bv, ld.at[0]),
        pltpu.make_async_copy(hist, x0, ld.at[1]),
        pltpu.make_async_copy(inv, iv, ld.at[2]),
    ]
    for step in range(2):
        for bb in range(2):
            loads.append(pltpu.make_async_copy(
                exc.at[step, 2 * xh + bb, pl.ds(z * zi, zi)], ev.at[step, bb], ld.at[3 + step * 2 + bb]))
    for copy in loads:
        copy.start()

    barrier = pltpu.get_barrier_semaphore()

    def greet(device):
        pl.semaphore_signal(barrier, inc=1, device_id=device, device_id_type=MESH)

    for d in range(1, K):
        greet((wrap(k + d, K), s, h))
    for d in range(1, 2 * S):
        other = wrap(e + d, 2 * S)
        greet((k, lax.div(other, 2), lax.rem(other, 2)))
    greet(at_x(3 - x))

    acc[32] = jnp.zeros((128, 128), F32)

    def products(tile):
        def body(g):
            total = acc[wrap(4 * g + 32, 33)]
            for c in range(4):
                c = 4 * g + c
                made = jnp.dot(bv[tab[c]], tile[tab[32 + c]], preferred_element_type=F32)
                total = made + total * tab[64 + c].astype(F32)
                acc[c] = total

        loop(8, body)

    loads[0].wait()
    loads[1].wait()
    products(x0)
    for copy in loads[2:]:
        copy.wait()
    pl.semaphore_wait(barrier, (K - 1) + (2 * S - 1) + 1)

    def row_block(xx, yy, bb):
        return 4 * (lax.rem(xx, 2) * Y + yy) + 2 * lax.div(xx, 2) + bb

    def first_stage(step):
        for i in range(4):
            dx = (i + 2) % 4
            xx = wrap(x + dx, 4)

            def fill_a(u):
                pa[step, xx, u] = acc[tab[96 + row_block(xx, u, 0)]].astype(BF16)

            loop(Y, fill_a)
            if dx:
                rcopy(pa.at[step, xx], ra.at[step, dx - 1], a1s.at[step, dx - 1], a1r.at[step, dx - 1], at_x(xx)).start()
            if i < Y:
                dy = (i + Y // 2) % Y
                yy = wrap(y + dy, Y)

                def fill_b(u):
                    pb[step, yy, u] = acc[tab[96 + row_block(u, yy, 1)]].astype(BF16)

                loop(4, fill_b)
                if dy:
                    rcopy(pb.at[step, yy], rb.at[step, dy - 1], b1s.at[step, dy - 1], b1r.at[step, dy - 1], at_y(yy)).start()

    def second_stage(step):
        for d in range(3):
            drain(ra.at[step, d], a1r.at[step, d])
        total = pa[step, x].astype(F32)
        for d in range(3):
            total += ra[step, d].astype(F32)
        qa[step] = total.astype(BF16)
        for dy in [Y // 2] + [d for d in range(1, Y) if d != Y // 2]:
            yy = wrap(y + dy, Y)
            rcopy(qa.at[step, yy], sa.at[step, dy - 1], a2s.at[step, dy - 1], a2r.at[step, dy - 1], at_y(yy)).start()
        for d in range(Y - 1):
            drain(rb.at[step, d], b1r.at[step, d])
        total = pb[step, y].astype(F32)
        for d in range(Y - 1):
            total += rb[step, d].astype(F32)
        qb[step] = total.astype(BF16)
        for dx in (2, 1, 3):
            xx = wrap(x + dx, 4)
            rcopy(qb.at[step, xx], sb.at[step, dx - 1], b2s.at[step, dx - 1], b2r.at[step, dx - 1], at_x(xx)).start()

    def far_first(i):
        return Z // 2 + (1 - 2 * lax.rem(i, 2)) * lax.div(i + 1, 2)

    def third_stage(step):
        for d in range(Y - 1):
            drain(sa.at[step, d], a2r.at[step, d])
        first = qa[step, y].astype(F32)
        for d in range(Y - 1):
            first += sa[step, d].astype(F32)
        for d in range(3):
            drain(sb.at[step, d], b2r.at[step, d])
        second = qb[step, x].astype(F32)
        for d in range(3):
            second += sb[step, d].astype(F32)
        both = jnp.concatenate([first.reshape(Z, zi, 128), second.reshape(Z, zi, 128)], axis=1)
        zs[step] = both.astype(BF16)

        def give(i):
            other = wrap(z + far_first(i), Z)
            rcopy(zs.at[step, other], zr.at[step, z], zss.at[step], zrs.at[step], (other * 2 + xh, s, h)).start()

        loop(Z - 1, give)

    def field(step):
        drain(zr.at[step, pl.ds(0, Z - 1)], zrs.at[step])
        zr[step, z] = zs[step, z]
        return jnp.sum(zr[step].astype(F32), axis=0)

    def gather(step, total):
        incident = jnp.concatenate([ev[step, 0].astype(F32), ev[step, 1].astype(F32)], axis=0)
        dv[step, xh * Z + z] = (incident - total).astype(BF16)
        here = dv.at[step, xh * Z + z]

        if step == 0:
            def give(i):
                other = wrap(z + far_first(i), Z)
                for half in (1 - xh, xh):
                    rcopy(here, here, gss.at[step], grs.at[step], (other * 2 + half, s, h)).start()

            loop(Z - 1, give)
            rcopy(here, here, gss.at[step], grs.at[step], (z * 2 + (1 - xh), s, h)).start()
        else:
            rcopy(here, here, gss.at[step], grs.at[step], (z * 2 + (1 - xh), s, h)).start()

            def hand(i):
                other = i + (z <= i).astype(jnp.int32)
                for half in (1 - xh, xh):
                    rcopy(here, here, gss.at[step], grs.at[step], (other * 2 + half, s, h)).start()

            loop(Z - 1, hand)

    def driven(step):
        drain(dv.at[step, pl.ds(0, K - 1)], grs.at[step])
        for half in range(2):
            chunk = dv[step, half * Z:(half + 1) * Z].astype(F32)
            for bb in range(2):
                dr[step, 2 * half + bb] = chunk[:, bb * zi:(bb + 1) * zi, :].reshape(128, 128).astype(BF16)
        pltpu.make_async_copy(dr.at[step], out.at[step], os.at[step]).start()

    first_stage(0)

    mine = pl.ds(4 * h, 4)

    @pl.when(k < K - 1)
    def _():
        rcopy(hist.at[mine], x1.at[mine], hs.at[0], hr.at[0], (k + 1, s, h)).start()

    @pl.when(k == 0)
    def _():
        def pack(c):
            pk[:, c] = bv[c].astype(F32).reshape(Z, zi, 128).astype(BF16)

        loop(32, pack)

        def give(i):
            other = 1 + i
            rcopy(pk.at[other], sl.at[h], cs.at[0], cr.at[0], (other * 2, s, h)).start()
            rcopy(key, kv.at[h], cs.at[1], cr.at[1], (other * 2, s, h)).start()

        loop(Z - 1, give)
        pltpu.make_async_copy(pk.at[0], sl.at[h], cr.at[0]).start()
        pltpu.make_async_copy(key, kv.at[h], cr.at[1]).start()

    second_stage(0)
    third_stage(0)

    @pl.when(k > 0)
    def _():
        drain(x1.at[mine], hr.at[0])
        rcopy(x1.at[mine], x1.at[mine], hs.at[1], hr.at[1], (k, s, 1 - h)).start()
        drain(x1.at[pl.ds(4 - 4 * h, 4)], hr.at[1])
        products(x1)

    @pl.when(k == 0)
    def _():
        def clear(c):
            acc[c] = jnp.zeros((128, 128), F32)

        loop(32, clear)

    first_stage(1)
    gather(0, field(0))

    @pl.when(xh == 0)
    def _():
        drain(sl.at[h], cr.at[0])
        drain(kv.at[h], cr.at[1])
        rcopy(sl.at[h], sl.at[h], cs.at[2], cr.at[0], (k + 1, s, h)).start()
        rcopy(kv.at[h], kv.at[h], cs.at[3], cr.at[1], (k + 1, s, h)).start()

    second_stage(1)

    @pl.when(xh == 1)
    def _():
        drain(sl.at[h], cr.at[0])
        drain(kv.at[h], cr.at[1])

    rcopy(sl.at[h], sl.at[h], cs.at[4], cr.at[2], (k, s, 1 - h)).start()
    rcopy(kv.at[h], kv.at[h], cs.at[5], cr.at[3], (k, s, 1 - h)).start()
    third_stage(1)

    drain(sl.at[1 - h], cr.at[2])
    drain(kv.at[1 - h], cr.at[3])
    rows, wide = S * 2 * zi, 32 * zi
    m = lax.broadcasted_iota(jnp.int32, (rows, wide), 0)
    n = lax.broadcasted_iota(jnp.int32, (rows, wide), 1)
    q = m // zi
    place = (4 * (q // 2) + 2 * xh + q % 2) * 8 + 4 * h
    same = (m % zi) == (n % zi)
    for half in range(2):
        slots = sl[half].astype(F32).reshape(wide, 128).astype(BF16)
        where = jnp.broadcast_to(kv[half, 0:1, :], (rows, wide))
        for jj in range(4):
            pick = jnp.where(same & (where == place + jj), 1.0, 0.0).astype(BF16)
            ad[half, :, jj * 128:(jj + 1) * 128] = jnp.dot(pick, slots, preferred_element_type=F32).astype(BF16)

    driven(0)
    for b in range(4):
        ov[b * 128:(b + 1) * 128] = jnp.dot(iv[b], dr[0, b], preferred_element_type=F32).astype(BF16)
    newest = ov[...]
    for half in range(2):
        made = jnp.dot(ad[half], newest, preferred_element_type=F32).astype(BF16)
        for other in range(S):
            us[other * 2 + half] = made[other * 2 * zi:(other + 1) * 2 * zi]

    for d in list(range(S, 2 * S)) + list(range(1, S)):
        other = wrap(e + d, 2 * S)
        rcopy(us.at[other], ur.at[e], uss.at[0], urs.at[0], (k, lax.div(other, 2), lax.rem(other, 2))).start()

    rest = field(1)
    drain(ur.at[pl.ds(0, 2 * S - 1)], urs.at[0])
    ur[e] = us[e]
    gather(1, rest + jnp.sum(ur[...].astype(F32), axis=0))
    driven(1)

    for step in range(2):
        for d in range(3):
            drain(pa.at[step, 0], a1s.at[step, d])
            drain(qb.at[step, 0], b2s.at[step, d])
        for d in range(Y - 1):
            drain(pb.at[step, 0], b1s.at[step, d])
            drain(qa.at[step, 0], a2s.at[step, d])
        drain(zs.at[step, pl.ds(0, Z - 1)], zss.at[step])
        drain(dv.at[step, pl.ds(0, K - 1)], gss.at[step])
    drain(us.at[pl.ds(0, 2 * S - 1)], uss.at[0])

    @pl.when(k < K - 1)
    def _():
        drain(x1.at[mine], hs.at[0])

    @pl.when(k > 0)
    def _():
        drain(x1.at[mine], hs.at[1])

    @pl.when(k == 0)
    def _():
        drain(bv.at[pl.ds(0, 32 - 32 // Z)], cs.at[0])
        drain(dv.at[0, pl.ds(0, 2 * Z - 2)], cs.at[1])

    @pl.when(xh == 0)
    def _():
        drain(sl.at[h], cs.at[2])
        drain(kv.at[h], cs.at[3])

    drain(sl.at[h], cs.at[4])
    drain(kv.at[h], cs.at[5])
    for step in range(2):
        pltpu.make_async_copy(dr.at[step], out.at[step], os.at[step]).wait()


def pin(array):
    return pltpu.with_memory_space_constraint(array, pltpu.HBM)


def shards(K, S, blocks, coords, counts, history, excitation, inverse):
    Y, Z = S // 2, K // 2
    zi = 128 // Z
    slots = lax.iota(jnp.int32, 32)
    places = coords[0, 0, 0]
    key = jnp.where(slots < counts[0, 0, 0], places[:, 0] * 8 + places[:, 1], 1 << 20)
    ahead = (key[None, :] < key[:, None]) | ((key[None, :] == key[:, None]) & (slots[None, :] < slots[:, None]))
    rank = jnp.sum(ahead.astype(jnp.int32), axis=1)
    chosen = rank[None, :] == slots[:, None]
    order = jnp.sum(jnp.where(chosen, slots[None, :], 0), axis=1)
    placed = jnp.sum(jnp.where(chosen, key[None, :], 0), axis=1)
    row = placed // 8
    before = jnp.sum(jnp.where(rank[None, :] == slots[:, None] - 1, key[None, :] // 8, 0), axis=1)
    keep = ((slots > 0) & (row == before)).astype(jnp.int32)
    last = jnp.max(jnp.where(key[None, :] // 8 == lax.iota(jnp.int32, 4 * S)[:, None], rank[None, :], -1), axis=1)
    last = jnp.where(last < 0, 32, last)
    tab = jnp.concatenate([order, placed % 8, keep, last])
    wide = jnp.broadcast_to(key[None, :, None], (8, 32, zi)).reshape(8, 32 * zi)
    dma = pltpu.SemaphoreType.DMA
    v = pltpu.VMEM
    scratch = [
        v((32, 128, 128), BF16), v((Z, 32, zi, 128), BF16), v((8, 128, 128), BF16), v((8, 128, 128), BF16), v((2, 2, zi, 128), BF16), v((4, 128, 128), BF16),
        v((33, 128, 128), F32), v((2, 4, 128, 128), BF16),
        v((2, 4, Y, 128, 128), BF16), v((2, Y, 4, 128, 128), BF16),
        v((2, 3, Y, 128, 128), BF16), v((2, Y - 1, 4, 128, 128), BF16),
        v((2, Y, 128, 128), BF16), v((2, 4, 128, 128), BF16),
        v((2, Y - 1, 128, 128), BF16), v((2, 3, 128, 128), BF16),
        v((2, Z, 2 * zi, 128), BF16), v((2, Z, 2 * zi, 128), BF16), v((2, K, 2 * zi, 128), BF16),
        v((2, 32, zi, 128), BF16), v((2, 8, 32 * zi), jnp.int32), v((2, S * 2 * zi, 512), BF16),
        v((2 * S, 2 * zi, 128), BF16), v((2 * S, 2 * zi, 128), BF16), v((512, 128), BF16),
        dma((7,)), dma((2, 3)), dma((2, 3)), dma((2, Y - 1)), dma((2, Y - 1)),
        dma((2, Y - 1)), dma((2, Y - 1)), dma((2, 3)), dma((2, 3)),
        dma((2,)), dma((2,)), dma((2,)), dma((2,)), dma((1,)), dma((1,)), dma((2,)), dma((2,)), dma((6,)), dma((4,)), dma((2,)),
    ]
    hbm = pl.BlockSpec(memory_space=pltpu.HBM)
    made = pl.pallas_call(
        functools.partial(kernel, K, Y),
        out_shape=jax.ShapeDtypeStruct((2, 4, 128, 128), BF16),
        in_specs=[pl.BlockSpec(memory_space=pltpu.SMEM), pl.BlockSpec(memory_space=pl.ANY)] + [hbm] * 4,
        out_specs=pl.BlockSpec(memory_space=pl.ANY),
        scratch_shapes=scratch,
        compiler_params=pltpu.CompilerParams(
            collective_id=0, has_side_effects=True, vmem_limit_bytes=40 * 1024 * 1024),
        name="march",
    )(
        tab, wide, pin(blocks[0, 0, 0]), pin(history[0].reshape(8, 128, 128)),
        pin(excitation[:, 0].reshape(2, 4, 128, 128)), pin(inverse[0]),
    )
    both = jnp.broadcast_to(inverse[0][None], made.shape)
    currents = jnp.einsum("nbij,nbjw->nbiw", both, made, preferred_element_type=F32)
    return currents.astype(BF16).reshape(2, 1, 512, 128)


def solution(mesh):
    placed = (
        P("delay", "src", "tgt", None, None, None),
        P("delay", "src", "tgt", None, None),
        P("delay", "src", "tgt"),
        P("delay", None, "src", None),
        P(None, "tgt", "src", None),
        P("tgt", "src", None, None),
    )
    return jax.shard_map(
        functools.partial(shards, mesh.shape["delay"], mesh.shape["src"]),
        mesh=mesh, in_specs=placed, out_specs=P(None, "tgt", "src", None), check_vma=False,
    )
```

```python
import functools

import jax
import jax.numpy as jnp
from jax import lax
from jax.experimental import pallas as pl
from jax.experimental.pallas import tpu as pltpu
from jax.sharding import PartitionSpec as P

MESH = pl.DeviceIdType.MESH
F32 = jnp.float32
BF16 = jnp.bfloat16


def rcopy(src, dst, send, recv, device):
    return pltpu.make_async_remote_copy(
        src_ref=src, dst_ref=dst, send_sem=send, recv_sem=recv, device_id=device, device_id_type=MESH
    )


def drain(ref, sem):
    pltpu.make_async_copy(ref, ref, sem).wait()


def wrap(value, size):
    return lax.rem(value, size)


def loop(count, body):
    def step(i, carry):
        body(i)
        return carry

    lax.fori_loop(0, count, step, 0)


def kernel(
    K, Y,
    tab, key, blocks, hist, exc, inv, out,
    bv, pk, x0, x1, ev, iv, acc, dr, pa, pb, ra, rb, qa, qb, sa, sb, zs, zr, dv, sl, kv, ad, us, ur, ov,
    ld, a1s, a1r, b1s, b1r, a2s, a2r, b2s, b2r, zss, zrs, gss, grs, uss, urs, hs, hr, cs, cr, os, known,
):
    k, s, h = lax.axis_index("delay"), lax.axis_index("src"), lax.axis_index("tgt")
    Z = K // 2
    S = 2 * Y
    zi = 128 // Z
    z, xh = lax.div(k, 2), lax.rem(k, 2)
    xl, y = lax.div(s, Y), lax.rem(s, Y)
    x = xh * 2 + xl
    e = s * 2 + h

    def at_x(other):
        return (z * 2 + lax.div(other, 2), lax.rem(other, 2) * Y + y, h)

    def at_y(other):
        return (k, xl * Y + other, h)

    loads = [
        pltpu.make_async_copy(blocks, bv, ld.at[0]),
        pltpu.make_async_copy(hist, x0, ld.at[1]),
        pltpu.make_async_copy(inv, iv, ld.at[2]),
    ]
    for step in range(2):
        for bb in range(2):
            loads.append(pltpu.make_async_copy(
                exc.at[step, 2 * xh + bb, pl.ds(z * zi, zi)], ev.at[step, bb], ld.at[3 + step * 2 + bb]))
    for copy in loads:
        copy.start()

    barrier = pltpu.get_barrier_semaphore()

    def greet(device):
        pl.semaphore_signal(barrier, inc=1, device_id=device, device_id_type=MESH)

    for d in range(1, 2 * S):
        other = wrap(e + d, 2 * S)
        greet((k, lax.div(other, 2), lax.rem(other, 2)))
    greet((k + 1 - 2 * xh, s, h))
    greet(at_x(3 - x))
    greet((wrap(k + 2 * xh - 1 + K, K), s, h))
    greet((wrap(k + 2, K), s, h))
    greet((wrap(k + K - 2, K), s, h))

    acc[32] = jnp.zeros((128, 128), F32)

    def products(tile):
        def body(g):
            total = acc[wrap(4 * g + 32, 33)]
            for c in range(4):
                c = 4 * g + c
                made = jnp.dot(bv[tab[c]], tile[tab[32 + c]], preferred_element_type=F32)
                total = made + total * tab[64 + c].astype(F32)
                acc[c] = total

        loop(8, body)

    pl.semaphore_wait(barrier, (2 * S - 1) + 5)

    def tell(turn):
        for d in (1 << turn, Z - (1 << turn)):
            pl.semaphore_signal(known.at[turn], inc=1, device_id=(wrap(z + d, Z) * 2 + xh, s, h), device_id_type=MESH)

    def heard(turn):
        pl.semaphore_wait(known.at[turn], 2)

    turns = max(Z // 2, 1).bit_length() - 1
    if turns > 0:
        tell(0)

    mine = pl.ds(4 * h, 4)

    @pl.when(k < K - 1)
    def _():
        rcopy(hist.at[mine], x1.at[mine], hs.at[0], hr.at[0], (k + 1, s, h)).start()

    loads[0].wait()
    loads[1].wait()
    products(x0)
    for copy in loads[2:]:
        copy.wait()

    def row_block(xx, yy, bb):
        return 4 * (lax.rem(xx, 2) * Y + yy) + 2 * lax.div(xx, 2) + bb

    def first_stage(step):
        for i in range(4):
            dx = (i + 2) % 4
            xx = wrap(x + dx, 4)

            def fill_a(u):
                pa[step, xx, u] = acc[tab[96 + row_block(xx, u, 0)]].astype(BF16)

            loop(Y, fill_a)
            if dx:
                rcopy(pa.at[step, xx], ra.at[step, dx - 1], a1s.at[step, dx - 1], a1r.at[step, dx - 1], at_x(xx)).start()
            if i < Y:
                dy = (i + Y // 2) % Y
                yy = wrap(y + dy, Y)

                def fill_b(u):
                    pb[step, yy, u] = acc[tab[96 + row_block(u, yy, 1)]].astype(BF16)

                loop(4, fill_b)
                if dy:
                    rcopy(pb.at[step, yy], rb.at[step, dy - 1], b1s.at[step, dy - 1], b1r.at[step, dy - 1], at_y(yy)).start()

    def second_stage(step):
        for d in range(3):
            drain(ra.at[step, d], a1r.at[step, d])
        total = pa[step, x].astype(F32)
        for d in range(3):
            total += ra[step, d].astype(F32)
        qa[step] = total.astype(BF16)
        for dy in [Y // 2] + [d for d in range(1, Y) if d != Y // 2]:
            yy = wrap(y + dy, Y)
            rcopy(qa.at[step, yy], sa.at[step, dy - 1], a2s.at[step, dy - 1], a2r.at[step, dy - 1], at_y(yy)).start()
        for d in range(Y - 1):
            drain(rb.at[step, d], b1r.at[step, d])
        total = pb[step, y].astype(F32)
        for d in range(Y - 1):
            total += rb[step, d].astype(F32)
        qb[step] = total.astype(BF16)
        for dx in (2, 1, 3):
            xx = wrap(x + dx, 4)
            rcopy(qb.at[step, xx], sb.at[step, dx - 1], b2s.at[step, dx - 1], b2r.at[step, dx - 1], at_x(xx)).start()

    def far_first(i):
        return Z // 2 + (1 - 2 * lax.rem(i, 2)) * lax.div(i + 1, 2)

    def third_stage(step):
        for d in range(Y - 1):
            drain(sa.at[step, d], a2r.at[step, d])
        first = qa[step, y].astype(F32)
        for d in range(Y - 1):
            first += sa[step, d].astype(F32)
        for d in range(3):
            drain(sb.at[step, d], b2r.at[step, d])
        second = qb[step, x].astype(F32)
        for d in range(3):
            second += sb[step, d].astype(F32)
        both = jnp.concatenate([first.reshape(Z, zi, 128), second.reshape(Z, zi, 128)], axis=1)
        zs[step] = both.astype(BF16)

        def give(i):
            other = wrap(z + far_first(i), Z)
            rcopy(zs.at[step, other], zr.at[step, z], zss.at[step], zrs.at[step], (other * 2 + xh, s, h)).start()

        loop(Z - 1, give)

    def field(step):
        drain(zr.at[step, pl.ds(0, Z - 1)], zrs.at[step])
        zr[step, z] = zs[step, z]
        return jnp.sum(zr[step].astype(F32), axis=0)

    def gather(step, total):
        incident = jnp.concatenate([ev[step, 0].astype(F32), ev[step, 1].astype(F32)], axis=0)
        dv[step, xh * Z + z] = (incident - total).astype(BF16)
        here = dv.at[step, xh * Z + z]

        if step == 0:
            def give(i):
                other = wrap(z + far_first(i), Z)
                for half in (1 - xh, xh):
                    rcopy(here, here, gss.at[step], grs.at[step], (other * 2 + half, s, h)).start()

            loop(Z - 1, give)
            rcopy(here, here, gss.at[step], grs.at[step], (z * 2 + (1 - xh), s, h)).start()
        else:
            rcopy(here, here, gss.at[step], grs.at[step], (z * 2 + (1 - xh), s, h)).start()

            def hand(i):
                other = i + (z <= i).astype(jnp.int32)
                for half in (1 - xh, xh):
                    rcopy(here, here, gss.at[step], grs.at[step], (other * 2 + half, s, h)).start()

            loop(Z - 1, hand)

    def driven(step):
        drain(dv.at[step, pl.ds(0, K - 1)], grs.at[step])
        for half in range(2):
            chunk = dv[step, half * Z:(half + 1) * Z].astype(F32)
            for bb in range(2):
                dr[step, 2 * half + bb] = chunk[:, bb * zi:(bb + 1) * zi, :].reshape(128, 128).astype(BF16)
        pltpu.make_async_copy(dr.at[step], out.at[step], os.at[step]).start()

    first_stage(0)

    if turns > 0:
        heard(0)
    if turns > 1:
        tell(1)

    @pl.when(k > 0)
    def _():
        drain(x1.at[mine], hr.at[0])
        rcopy(x1.at[mine], x1.at[mine], hs.at[1], hr.at[1], (k, s, 1 - h)).start()

    if turns > 1:
        heard(1)
    if turns > 2:
        tell(2)
    second_stage(0)
    if turns > 2:
        heard(2)

    @pl.when(k > 0)
    def _():
        drain(x1.at[pl.ds(4 - 4 * h, 4)], hr.at[1])
        products(x1)

    @pl.when(k == 0)
    def _():
        def clear(c):
            acc[c] = jnp.zeros((128, 128), F32)

        loop(32, clear)

    third_stage(0)

    @pl.when(k == 0)
    def _():
        def pack(c):
            pk[:, c] = bv[c].astype(F32).reshape(Z, zi, 128).astype(BF16)

        loop(32, pack)

        def give(i):
            other = 1 + i
            rcopy(pk.at[other], sl.at[h], cs.at[0], cr.at[0], (other * 2, s, h)).start()
            rcopy(key, kv.at[h], cs.at[1], cr.at[1], (other * 2, s, h)).start()

        loop(Z - 1, give)
        pltpu.make_async_copy(pk.at[0], sl.at[h], cr.at[0]).start()
        pltpu.make_async_copy(key, kv.at[h], cr.at[1]).start()

    first_stage(1)
    gather(0, field(0))

    @pl.when(xh == 0)
    def _():
        drain(sl.at[h], cr.at[0])
        drain(kv.at[h], cr.at[1])
        rcopy(sl.at[h], sl.at[h], cs.at[2], cr.at[0], (k + 1, s, h)).start()
        rcopy(kv.at[h], kv.at[h], cs.at[3], cr.at[1], (k + 1, s, h)).start()

    second_stage(1)

    @pl.when(xh == 1)
    def _():
        drain(sl.at[h], cr.at[0])
        drain(kv.at[h], cr.at[1])

    rcopy(sl.at[h], sl.at[h], cs.at[4], cr.at[2], (k, s, 1 - h)).start()
    rcopy(kv.at[h], kv.at[h], cs.at[5], cr.at[3], (k, s, 1 - h)).start()
    third_stage(1)

    drain(sl.at[1 - h], cr.at[2])
    drain(kv.at[1 - h], cr.at[3])
    rows, wide = S * 2 * zi, 32 * zi
    m = lax.broadcasted_iota(jnp.int32, (rows, wide), 0)
    n = lax.broadcasted_iota(jnp.int32, (rows, wide), 1)
    q = m // zi
    place = (4 * (q // 2) + 2 * xh + q % 2) * 8 + 4 * h
    same = (m % zi) == (n % zi)
    for half in range(2):
        slots = sl[half].astype(F32).reshape(wide, 128).astype(BF16)
        where = jnp.broadcast_to(kv[half, 0:1, :], (rows, wide))
        for jj in range(4):
            pick = jnp.where(same & (where == place + jj), 1.0, 0.0).astype(BF16)
            ad[half, :, jj * 128:(jj + 1) * 128] = jnp.dot(pick, slots, preferred_element_type=F32).astype(BF16)

    driven(0)
    for b in range(4):
        ov[b * 128:(b + 1) * 128] = jnp.dot(iv[b], dr[0, b], preferred_element_type=F32).astype(BF16)
    newest = ov[...]
    for half in range(2):
        made = jnp.dot(ad[half], newest, preferred_element_type=F32).astype(BF16)
        for other in range(S):
            us[other * 2 + half] = made[other * 2 * zi:(other + 1) * 2 * zi]

    for d in list(range(S, 2 * S)) + list(range(1, S)):
        other = wrap(e + d, 2 * S)
        rcopy(us.at[other], ur.at[e], uss.at[0], urs.at[0], (k, lax.div(other, 2), lax.rem(other, 2))).start()

    rest = field(1)
    drain(ur.at[pl.ds(0, 2 * S - 1)], urs.at[0])
    ur[e] = us[e]
    gather(1, rest + jnp.sum(ur[...].astype(F32), axis=0))
    driven(1)

    for step in range(2):
        for d in range(3):
            drain(pa.at[step, 0], a1s.at[step, d])
            drain(qb.at[step, 0], b2s.at[step, d])
        for d in range(Y - 1):
            drain(pb.at[step, 0], b1s.at[step, d])
            drain(qa.at[step, 0], a2s.at[step, d])
        drain(zs.at[step, pl.ds(0, Z - 1)], zss.at[step])
        drain(dv.at[step, pl.ds(0, K - 1)], gss.at[step])
    drain(us.at[pl.ds(0, 2 * S - 1)], uss.at[0])

    @pl.when(k < K - 1)
    def _():
        drain(x1.at[mine], hs.at[0])

    @pl.when(k > 0)
    def _():
        drain(x1.at[mine], hs.at[1])

    @pl.when(k == 0)
    def _():
        drain(bv.at[pl.ds(0, 32 - 32 // Z)], cs.at[0])
        drain(dv.at[0, pl.ds(0, 2 * Z - 2)], cs.at[1])

    @pl.when(xh == 0)
    def _():
        drain(sl.at[h], cs.at[2])
        drain(kv.at[h], cs.at[3])

    drain(sl.at[h], cs.at[4])
    drain(kv.at[h], cs.at[5])
    for step in range(2):
        pltpu.make_async_copy(dr.at[step], out.at[step], os.at[step]).wait()


def pin(array):
    return pltpu.with_memory_space_constraint(array, pltpu.HBM)


def shards(K, S, blocks, coords, counts, history, excitation, inverse):
    Y, Z = S // 2, K // 2
    zi = 128 // Z
    slots = lax.iota(jnp.int32, 32)
    places = coords[0, 0, 0]
    key = jnp.where(slots < counts[0, 0, 0], places[:, 0] * 8 + places[:, 1], 1 << 20)
    ahead = (key[None, :] < key[:, None]) | ((key[None, :] == key[:, None]) & (slots[None, :] < slots[:, None]))
    rank = jnp.sum(ahead.astype(jnp.int32), axis=1)
    chosen = rank[None, :] == slots[:, None]
    order = jnp.sum(jnp.where(chosen, slots[None, :], 0), axis=1)
    placed = jnp.sum(jnp.where(chosen, key[None, :], 0), axis=1)
    row = placed // 8
    before = jnp.sum(jnp.where(rank[None, :] == slots[:, None] - 1, key[None, :] // 8, 0), axis=1)
    keep = ((slots > 0) & (row == before)).astype(jnp.int32)
    last = jnp.max(jnp.where(key[None, :] // 8 == lax.iota(jnp.int32, 4 * S)[:, None], rank[None, :], -1), axis=1)
    last = jnp.where(last < 0, 32, last)
    tab = jnp.concatenate([order, placed % 8, keep, last])
    wide = jnp.broadcast_to(key[None, :, None], (8, 32, zi)).reshape(8, 32 * zi)
    dma = pltpu.SemaphoreType.DMA
    v = pltpu.VMEM
    scratch = [
        v((32, 128, 128), BF16), v((Z, 32, zi, 128), BF16), v((8, 128, 128), BF16), v((8, 128, 128), BF16), v((2, 2, zi, 128), BF16), v((4, 128, 128), BF16),
        v((33, 128, 128), F32), v((2, 4, 128, 128), BF16),
        v((2, 4, Y, 128, 128), BF16), v((2, Y, 4, 128, 128), BF16),
        v((2, 3, Y, 128, 128), BF16), v((2, Y - 1, 4, 128, 128), BF16),
        v((2, Y, 128, 128), BF16), v((2, 4, 128, 128), BF16),
        v((2, Y - 1, 128, 128), BF16), v((2, 3, 128, 128), BF16),
        v((2, Z, 2 * zi, 128), BF16), v((2, Z, 2 * zi, 128), BF16), v((2, K, 2 * zi, 128), BF16),
        v((2, 32, zi, 128), BF16), v((2, 8, 32 * zi), jnp.int32), v((2, S * 2 * zi, 512), BF16),
        v((2 * S, 2 * zi, 128), BF16), v((2 * S, 2 * zi, 128), BF16), v((512, 128), BF16),
        dma((7,)), dma((2, 3)), dma((2, 3)), dma((2, Y - 1)), dma((2, Y - 1)),
        dma((2, Y - 1)), dma((2, Y - 1)), dma((2, 3)), dma((2, 3)),
        dma((2,)), dma((2,)), dma((2,)), dma((2,)), dma((1,)), dma((1,)), dma((2,)), dma((2,)), dma((6,)), dma((4,)), dma((2,)),
        pltpu.SemaphoreType.REGULAR((4,)),
    ]
    hbm = pl.BlockSpec(memory_space=pltpu.HBM)
    made = pl.pallas_call(
        functools.partial(kernel, K, Y),
        out_shape=jax.ShapeDtypeStruct((2, 4, 128, 128), BF16),
        in_specs=[pl.BlockSpec(memory_space=pltpu.SMEM), pl.BlockSpec(memory_space=pl.ANY)] + [hbm] * 4,
        out_specs=pl.BlockSpec(memory_space=pl.ANY),
        scratch_shapes=scratch,
        compiler_params=pltpu.CompilerParams(
            collective_id=0, has_side_effects=True, vmem_limit_bytes=40 * 1024 * 1024),
        name="march",
    )(
        tab, wide, pin(blocks[0, 0, 0]), pin(history[0].reshape(8, 128, 128)),
        pin(excitation[:, 0].reshape(2, 4, 128, 128)), pin(inverse[0]),
    )
    both = jnp.broadcast_to(inverse[0][None], made.shape)
    currents = jnp.einsum("nbij,nbjw->nbiw", both, made, preferred_element_type=F32)
    return currents.astype(BF16).reshape(2, 1, 512, 128)


def solution(mesh):
    placed = (
        P("delay", "src", "tgt", None, None, None),
        P("delay", "src", "tgt", None, None),
        P("delay", "src", "tgt"),
        P("delay", None, "src", None),
        P(None, "tgt", "src", None),
        P("tgt", "src", None, None),
    )
    return jax.shard_map(
        functools.partial(shards, mesh.shape["delay"], mesh.shape["src"]),
        mesh=mesh, in_specs=placed, out_specs=P(None, "tgt", "src", None), check_vma=False,
    )
```

```python
import functools

import jax
import jax.numpy as jnp
from jax import lax
from jax.experimental import pallas as pl
from jax.experimental.pallas import tpu as pltpu
from jax.sharding import PartitionSpec as P

MESH = pl.DeviceIdType.MESH
F32 = jnp.float32
BF16 = jnp.bfloat16


def rcopy(src, dst, send, recv, device):
    return pltpu.make_async_remote_copy(
        src_ref=src, dst_ref=dst, send_sem=send, recv_sem=recv, device_id=device, device_id_type=MESH
    )


def drain(ref, sem):
    pltpu.make_async_copy(ref, ref, sem).wait()


def wrap(value, size):
    return lax.rem(value, size)


def loop(count, body):
    def step(i, carry):
        body(i)
        return carry

    lax.fori_loop(0, count, step, 0)


def kernel(
    K, Y,
    tab, key, blocks, hist, exc, inv, out,
    bv, pk, x0, x1, ev, iv, acc, dr, pa, pb, ra, rb, qa, qb, sa, sb, zs, zr, dv, sl, kv, ad, us, ur, ov,
    ld, a1s, a1r, b1s, b1r, a2s, a2r, b2s, b2r, zss, zrs, gss, grs, uss, urs, hs, hr, cs, cr, os, known,
):
    k, s, h = lax.axis_index("delay"), lax.axis_index("src"), lax.axis_index("tgt")
    Z = K // 2
    S = 2 * Y
    zi = 128 // Z
    z, xh = lax.div(k, 2), lax.rem(k, 2)
    xl, y = lax.div(s, Y), lax.rem(s, Y)
    x = xh * 2 + xl
    e = s * 2 + h

    def at_x(other):
        return (z * 2 + lax.div(other, 2), lax.rem(other, 2) * Y + y, h)

    def at_y(other):
        return (k, xl * Y + other, h)

    loads = [
        pltpu.make_async_copy(blocks, bv, ld.at[0]),
        pltpu.make_async_copy(hist, x0, ld.at[1]),
        pltpu.make_async_copy(inv, iv, ld.at[2]),
    ]
    for step in range(2):
        for bb in range(2):
            loads.append(pltpu.make_async_copy(
                exc.at[step, 2 * xh + bb, pl.ds(z * zi, zi)], ev.at[step, bb], ld.at[3 + step * 2 + bb]))
    for copy in loads:
        copy.start()

    barrier = pltpu.get_barrier_semaphore()

    def greet(device):
        pl.semaphore_signal(barrier, inc=1, device_id=device, device_id_type=MESH)

    for d in range(1, 2 * S):
        other = wrap(e + d, 2 * S)
        greet((k, lax.div(other, 2), lax.rem(other, 2)))
    greet((k + 1 - 2 * xh, s, h))
    greet(at_x(3 - x))
    greet((wrap(k + 2 * xh - 1 + K, K), s, h))
    greet((wrap(k + 2, K), s, h))
    greet((wrap(k + K - 2, K), s, h))

    acc[32] = jnp.zeros((128, 128), F32)

    def products(tile):
        def body(g):
            total = acc[wrap(4 * g + 32, 33)]
            for c in range(4):
                c = 4 * g + c
                made = jnp.dot(bv[tab[c]], tile[tab[32 + c]], preferred_element_type=F32)
                total = made + total * tab[64 + c].astype(F32)
                acc[c] = total

        loop(8, body)

    pl.semaphore_wait(barrier, (2 * S - 1) + 5)

    def tell(turn):
        for d in (1 << turn, Z - (1 << turn)):
            pl.semaphore_signal(known.at[turn], inc=1, device_id=(wrap(z + d, Z) * 2 + xh, s, h), device_id_type=MESH)

    def heard(turn):
        pl.semaphore_wait(known.at[turn], 2)

    turns = max(Z // 2, 1).bit_length() - 1
    if turns > 0:
        tell(0)

    mine = pl.ds(4 * h, 4)

    @pl.when(k < K - 1)
    def _():
        rcopy(hist.at[mine], x1.at[mine], hs.at[0], hr.at[0], (k + 1, s, h)).start()

    loads[0].wait()
    loads[1].wait()
    products(x0)
    for copy in loads[2:]:
        copy.wait()

    def row_block(xx, yy, bb):
        return 4 * (lax.rem(xx, 2) * Y + yy) + 2 * lax.div(xx, 2) + bb

    def first_stage(step):
        for i in range(4):
            dx = (i + 2) % 4
            xx = wrap(x + dx, 4)

            def fill_a(u):
                pa[step, xx, u] = acc[tab[96 + row_block(xx, u, 0)]].astype(BF16)

            loop(Y, fill_a)
            if dx:
                rcopy(pa.at[step, xx], ra.at[step, dx - 1], a1s.at[step, dx - 1], a1r.at[step, dx - 1], at_x(xx)).start()
            if i < Y:
                dy = (i + Y // 2) % Y
                yy = wrap(y + dy, Y)

                def fill_b(u):
                    pb[step, yy, u] = acc[tab[96 + row_block(u, yy, 1)]].astype(BF16)

                loop(4, fill_b)
                if dy:
                    rcopy(pb.at[step, yy], rb.at[step, dy - 1], b1s.at[step, dy - 1], b1r.at[step, dy - 1], at_y(yy)).start()

    def second_stage(step):
        for d in range(3):
            drain(ra.at[step, d], a1r.at[step, d])
        total = pa[step, x].astype(F32)
        for d in range(3):
            total += ra[step, d].astype(F32)
        qa[step] = total.astype(BF16)
        for dy in [Y // 2] + [d for d in range(1, Y) if d != Y // 2]:
            yy = wrap(y + dy, Y)
            rcopy(qa.at[step, yy], sa.at[step, dy - 1], a2s.at[step, dy - 1], a2r.at[step, dy - 1], at_y(yy)).start()
        for d in range(Y - 1):
            drain(rb.at[step, d], b1r.at[step, d])
        total = pb[step, y].astype(F32)
        for d in range(Y - 1):
            total += rb[step, d].astype(F32)
        qb[step] = total.astype(BF16)
        for dx in (2, 1, 3):
            xx = wrap(x + dx, 4)
            rcopy(qb.at[step, xx], sb.at[step, dx - 1], b2s.at[step, dx - 1], b2r.at[step, dx - 1], at_x(xx)).start()

    def far_first(i):
        return Z // 2 + (1 - 2 * lax.rem(i, 2)) * lax.div(i + 1, 2)

    def third_stage(step):
        for d in range(Y - 1):
            drain(sa.at[step, d], a2r.at[step, d])
        first = qa[step, y].astype(F32)
        for d in range(Y - 1):
            first += sa[step, d].astype(F32)
        for d in range(3):
            drain(sb.at[step, d], b2r.at[step, d])
        second = qb[step, x].astype(F32)
        for d in range(3):
            second += sb[step, d].astype(F32)
        both = jnp.concatenate([first.reshape(Z, zi, 128), second.reshape(Z, zi, 128)], axis=1)
        zs[step] = both.astype(BF16)

        def give(i):
            other = wrap(z + far_first(i), Z)
            rcopy(zs.at[step, other], zr.at[step, z], zss.at[step], zrs.at[step], (other * 2 + xh, s, h)).start()

        loop(Z - 1, give)

    def field(step):
        drain(zr.at[step, pl.ds(0, Z - 1)], zrs.at[step])
        zr[step, z] = zs[step, z]
        return jnp.sum(zr[step].astype(F32), axis=0)

    def gather(step, total):
        incident = jnp.concatenate([ev[step, 0].astype(F32), ev[step, 1].astype(F32)], axis=0)
        dv[step, xh * Z + z] = (incident - total).astype(BF16)
        here = dv.at[step, xh * Z + z]

        if step == 0:
            def give(i):
                other = wrap(z + far_first(i), Z)
                for half in (1 - xh, xh):
                    rcopy(here, here, gss.at[step], grs.at[step], (other * 2 + half, s, h)).start()

            loop(Z - 1, give)
            rcopy(here, here, gss.at[step], grs.at[step], (z * 2 + (1 - xh), s, h)).start()
        else:
            rcopy(here, here, gss.at[step], grs.at[step], (z * 2 + (1 - xh), s, h)).start()

            def hand(i):
                other = i + (z <= i).astype(jnp.int32)
                for half in (1 - xh, xh):
                    rcopy(here, here, gss.at[step], grs.at[step], (other * 2 + half, s, h)).start()

            loop(Z - 1, hand)

    def driven(step):
        drain(dv.at[step, pl.ds(0, K - 1)], grs.at[step])
        for half in range(2):
            chunk = dv[step, half * Z:(half + 1) * Z].astype(F32)
            for bb in range(2):
                dr[step, 2 * half + bb] = chunk[:, bb * zi:(bb + 1) * zi, :].reshape(128, 128).astype(BF16)
        pltpu.make_async_copy(dr.at[step], out.at[step], os.at[step]).start()

    first_stage(0)

    @pl.when(k == 0)
    def _():
        def pack(c):
            pk[:, c] = bv[c].astype(F32).reshape(Z, zi, 128).astype(BF16)

        loop(32, pack)

    def scatter(near, far):
        @pl.when(k == 0)
        def _():
            if near == 0:
                pltpu.make_async_copy(pk.at[0], sl.at[h], cr.at[0]).start()
                pltpu.make_async_copy(key, kv.at[h], cr.at[1]).start()
            for d in range(near + 1, far + 1):
                for other in sorted({d, Z - d}):
                    there = (other * 2 + 0, s, h)
                    rcopy(pk.at[other], sl.at[h], cs.at[0], cr.at[0], there).start()
                    rcopy(key, kv.at[h], cs.at[1], cr.at[1], there).start()

    scatter(0, 1)
    for turn in range(turns):
        heard(turn)
        if turn + 1 < turns:
            tell(turn + 1)
        scatter(1 << turn, 2 << turn)

    @pl.when(k > 0)
    def _():
        drain(x1.at[mine], hr.at[0])
        rcopy(x1.at[mine], x1.at[mine], hs.at[1], hr.at[1], (k, s, 1 - h)).start()

    second_stage(0)

    @pl.when(k > 0)
    def _():
        drain(x1.at[pl.ds(4 - 4 * h, 4)], hr.at[1])
        products(x1)

    @pl.when(k == 0)
    def _():
        def clear(c):
            acc[c] = jnp.zeros((128, 128), F32)

        loop(32, clear)

    third_stage(0)
    first_stage(1)
    gather(0, field(0))

    @pl.when(xh == 0)
    def _():
        drain(sl.at[h], cr.at[0])
        drain(kv.at[h], cr.at[1])
        rcopy(sl.at[h], sl.at[h], cs.at[2], cr.at[0], (k + 1 - 2 * xh, s, h)).start()
        rcopy(kv.at[h], kv.at[h], cs.at[3], cr.at[1], (k + 1 - 2 * xh, s, h)).start()

    second_stage(1)

    @pl.when(xh != 0)
    def _():
        drain(sl.at[h], cr.at[0])
        drain(kv.at[h], cr.at[1])

    rcopy(sl.at[h], sl.at[h], cs.at[4], cr.at[2], (k, s, 1 - h)).start()
    rcopy(kv.at[h], kv.at[h], cs.at[5], cr.at[3], (k, s, 1 - h)).start()
    third_stage(1)

    drain(sl.at[1 - h], cr.at[2])
    drain(kv.at[1 - h], cr.at[3])
    rows, wide = S * 2 * zi, 32 * zi
    m = lax.broadcasted_iota(jnp.int32, (rows, wide), 0)
    n = lax.broadcasted_iota(jnp.int32, (rows, wide), 1)
    q = m // zi
    place = (4 * (q // 2) + 2 * xh + q % 2) * 8 + 4 * h
    same = (m % zi) == (n % zi)
    for half in range(2):
        slots = sl[half].astype(F32).reshape(wide, 128).astype(BF16)
        where = jnp.broadcast_to(kv[half, 0:1, :], (rows, wide))
        for jj in range(4):
            pick = jnp.where(same & (where == place + jj), 1.0, 0.0).astype(BF16)
            ad[half, :, jj * 128:(jj + 1) * 128] = jnp.dot(pick, slots, preferred_element_type=F32).astype(BF16)

    driven(0)
    for b in range(4):
        ov[b * 128:(b + 1) * 128] = jnp.dot(iv[b], dr[0, b], preferred_element_type=F32).astype(BF16)
    newest = ov[...]
    for half in range(2):
        made = jnp.dot(ad[half], newest, preferred_element_type=F32).astype(BF16)
        for other in range(S):
            us[other * 2 + half] = made[other * 2 * zi:(other + 1) * 2 * zi]

    for d in list(range(S, 2 * S)) + list(range(1, S)):
        other = wrap(e + d, 2 * S)
        rcopy(us.at[other], ur.at[e], uss.at[0], urs.at[0], (k, lax.div(other, 2), lax.rem(other, 2))).start()

    rest = field(1)
    drain(ur.at[pl.ds(0, 2 * S - 1)], urs.at[0])
    ur[e] = us[e]
    gather(1, rest + jnp.sum(ur[...].astype(F32), axis=0))
    driven(1)

    for step in range(2):
        for d in range(3):
            drain(pa.at[step, 0], a1s.at[step, d])
            drain(qb.at[step, 0], b2s.at[step, d])
        for d in range(Y - 1):
            drain(pb.at[step, 0], b1s.at[step, d])
            drain(qa.at[step, 0], a2s.at[step, d])
        drain(zs.at[step, pl.ds(0, Z - 1)], zss.at[step])
        drain(dv.at[step, pl.ds(0, K - 1)], gss.at[step])
    drain(us.at[pl.ds(0, 2 * S - 1)], uss.at[0])

    @pl.when(k < K - 1)
    def _():
        drain(x1.at[mine], hs.at[0])

    @pl.when(k > 0)
    def _():
        drain(x1.at[mine], hs.at[1])

    @pl.when(k == 0)
    def _():
        drain(bv.at[pl.ds(0, 32 - 32 // Z)], cs.at[0])
        drain(dv.at[0, pl.ds(0, 2 * Z - 2)], cs.at[1])

    @pl.when(xh == 0)
    def _():
        drain(sl.at[h], cs.at[2])
        drain(kv.at[h], cs.at[3])

    drain(sl.at[h], cs.at[4])
    drain(kv.at[h], cs.at[5])
    for step in range(2):
        pltpu.make_async_copy(dr.at[step], out.at[step], os.at[step]).wait()


def pin(array):
    return pltpu.with_memory_space_constraint(array, pltpu.HBM)


def shards(K, S, blocks, coords, counts, history, excitation, inverse):
    Y, Z = S // 2, K // 2
    zi = 128 // Z
    slots = lax.iota(jnp.int32, 32)
    places = coords[0, 0, 0]
    key = jnp.where(slots < counts[0, 0, 0], places[:, 0] * 8 + places[:, 1], 1 << 20)
    ahead = (key[None, :] < key[:, None]) | ((key[None, :] == key[:, None]) & (slots[None, :] < slots[:, None]))
    rank = jnp.sum(ahead.astype(jnp.int32), axis=1)
    chosen = rank[None, :] == slots[:, None]
    order = jnp.sum(jnp.where(chosen, slots[None, :], 0), axis=1)
    placed = jnp.sum(jnp.where(chosen, key[None, :], 0), axis=1)
    row = placed // 8
    before = jnp.sum(jnp.where(rank[None, :] == slots[:, None] - 1, key[None, :] // 8, 0), axis=1)
    keep = ((slots > 0) & (row == before)).astype(jnp.int32)
    last = jnp.max(jnp.where(key[None, :] // 8 == lax.iota(jnp.int32, 4 * S)[:, None], rank[None, :], -1), axis=1)
    last = jnp.where(last < 0, 32, last)
    tab = jnp.concatenate([order, placed % 8, keep, last])
    wide = jnp.broadcast_to(key[None, :, None], (8, 32, zi)).reshape(8, 32 * zi)
    dma = pltpu.SemaphoreType.DMA
    v = pltpu.VMEM
    scratch = [
        v((32, 128, 128), BF16), v((Z, 32, zi, 128), BF16), v((8, 128, 128), BF16), v((8, 128, 128), BF16), v((2, 2, zi, 128), BF16), v((4, 128, 128), BF16),
        v((33, 128, 128), F32), v((2, 4, 128, 128), BF16),
        v((2, 4, Y, 128, 128), BF16), v((2, Y, 4, 128, 128), BF16),
        v((2, 3, Y, 128, 128), BF16), v((2, Y - 1, 4, 128, 128), BF16),
        v((2, Y, 128, 128), BF16), v((2, 4, 128, 128), BF16),
        v((2, Y - 1, 128, 128), BF16), v((2, 3, 128, 128), BF16),
        v((2, Z, 2 * zi, 128), BF16), v((2, Z, 2 * zi, 128), BF16), v((2, K, 2 * zi, 128), BF16),
        v((2, 32, zi, 128), BF16), v((2, 8, 32 * zi), jnp.int32), v((2, S * 2 * zi, 512), BF16),
        v((2 * S, 2 * zi, 128), BF16), v((2 * S, 2 * zi, 128), BF16), v((512, 128), BF16),
        dma((7,)), dma((2, 3)), dma((2, 3)), dma((2, Y - 1)), dma((2, Y - 1)),
        dma((2, Y - 1)), dma((2, Y - 1)), dma((2, 3)), dma((2, 3)),
        dma((2,)), dma((2,)), dma((2,)), dma((2,)), dma((1,)), dma((1,)), dma((2,)), dma((2,)), dma((6,)), dma((4,)), dma((2,)),
        pltpu.SemaphoreType.REGULAR((4,)),
    ]
    hbm = pl.BlockSpec(memory_space=pltpu.HBM)
    made = pl.pallas_call(
        functools.partial(kernel, K, Y),
        out_shape=jax.ShapeDtypeStruct((2, 4, 128, 128), BF16),
        in_specs=[pl.BlockSpec(memory_space=pltpu.SMEM), pl.BlockSpec(memory_space=pl.ANY)] + [hbm] * 4,
        out_specs=pl.BlockSpec(memory_space=pl.ANY),
        scratch_shapes=scratch,
        compiler_params=pltpu.CompilerParams(
            collective_id=0, has_side_effects=True, vmem_limit_bytes=40 * 1024 * 1024),
        name="march",
    )(
        tab, wide, pin(blocks[0, 0, 0]), pin(history[0].reshape(8, 128, 128)),
        pin(excitation[:, 0].reshape(2, 4, 128, 128)), pin(inverse[0]),
    )
    both = jnp.broadcast_to(inverse[0][None], made.shape)
    currents = jnp.einsum("nbij,nbjw->nbiw", both, made, preferred_element_type=F32)
    return currents.astype(BF16).reshape(2, 1, 512, 128)


def solution(mesh):
    placed = (
        P("delay", "src", "tgt", None, None, None),
        P("delay", "src", "tgt", None, None),
        P("delay", "src", "tgt"),
        P("delay", None, "src", None),
        P(None, "tgt", "src", None),
        P("tgt", "src", None, None),
    )
    return jax.shard_map(
        functools.partial(shards, mesh.shape["delay"], mesh.shape["src"]),
        mesh=mesh, in_specs=placed, out_specs=P(None, "tgt", "src", None), check_vma=False,
    )
```

```python
import functools

import jax
import jax.numpy as jnp
from jax import lax
from jax.experimental import pallas as pl
from jax.experimental.pallas import tpu as pltpu
from jax.sharding import PartitionSpec as P

MESH = pl.DeviceIdType.MESH
F32 = jnp.float32
BF16 = jnp.bfloat16


def rcopy(src, dst, send, recv, device):
    return pltpu.make_async_remote_copy(
        src_ref=src, dst_ref=dst, send_sem=send, recv_sem=recv, device_id=device, device_id_type=MESH
    )


def drain(ref, sem):
    pltpu.make_async_copy(ref, ref, sem).wait()


def wrap(value, size):
    return lax.rem(value, size)


def loop(count, body):
    def step(i, carry):
        body(i)
        return carry

    lax.fori_loop(0, count, step, 0)


def kernel(
    K, Y,
    tab, key, blocks, hist, exc, inv, out,
    bv, pk, x0, x1, ev, iv, acc, dr, pa, pb, ra, rb, qa, qb, sa, sb, zs, zr, dv, sl, kv, ad, us, ur, ov,
    ld, a1s, a1r, b1s, b1r, a2s, a2r, b2s, b2r, zss, zrs, gss, grs, uss, urs, hs, hr, cs, cr, os, known,
):
    k, s, h = lax.axis_index("delay"), lax.axis_index("src"), lax.axis_index("tgt")
    Z = K // 2
    S = 2 * Y
    zi = 128 // Z
    z, xh = lax.div(k, 2), lax.rem(k, 2)
    xl, y = lax.div(s, Y), lax.rem(s, Y)
    x = xh * 2 + xl
    e = s * 2 + h

    def at_x(other):
        return (z * 2 + lax.div(other, 2), lax.rem(other, 2) * Y + y, h)

    def at_y(other):
        return (k, xl * Y + other, h)

    loads = [
        pltpu.make_async_copy(blocks, bv, ld.at[0]),
        pltpu.make_async_copy(hist, x0, ld.at[1]),
        pltpu.make_async_copy(inv, iv, ld.at[2]),
    ]
    for step in range(2):
        for bb in range(2):
            loads.append(pltpu.make_async_copy(
                exc.at[step, 2 * xh + bb, pl.ds(z * zi, zi)], ev.at[step, bb], ld.at[3 + step * 2 + bb]))
    for copy in loads:
        copy.start()

    barrier = pltpu.get_barrier_semaphore()

    def greet(device):
        pl.semaphore_signal(barrier, inc=1, device_id=device, device_id_type=MESH)

    for d in range(1, 2 * S):
        other = wrap(e + d, 2 * S)
        greet((k, lax.div(other, 2), lax.rem(other, 2)))
    greet((k + 1 - 2 * xh, s, h))
    greet(at_x(3 - x))
    greet((wrap(k + 2 * xh - 1 + K, K), s, h))
    greet((wrap(k + 2, K), s, h))
    greet((wrap(k + K - 2, K), s, h))

    acc[32] = jnp.zeros((128, 128), F32)

    def products(tile):
        def body(g):
            total = acc[wrap(4 * g + 32, 33)]
            for c in range(4):
                c = 4 * g + c
                made = jnp.dot(bv[tab[c]], tile[tab[32 + c]], preferred_element_type=F32)
                total = made + total * tab[64 + c].astype(F32)
                acc[c] = total

        loop(8, body)


    loads[0].wait()
    loads[1].wait()
    products(x0)
    pl.semaphore_wait(barrier, (2 * S - 1) + 5)

    def tell(turn):
        for d in (1 << turn, Z - (1 << turn)):
            pl.semaphore_signal(known.at[turn], inc=1, device_id=(wrap(z + d, Z) * 2 + xh, s, h), device_id_type=MESH)

    def heard(turn):
        pl.semaphore_wait(known.at[turn], 2)

    turns = max(Z // 2, 1).bit_length() - 1
    if turns > 0:
        tell(0)

    mine = pl.ds(4 * h, 4)

    @pl.when(k < K - 1)
    def _():
        rcopy(hist.at[mine], x1.at[mine], hs.at[0], hr.at[0], (k + 1, s, h)).start()

    for copy in loads[2:]:
        copy.wait()

    def row_block(xx, yy, bb):
        return 4 * (lax.rem(xx, 2) * Y + yy) + 2 * lax.div(xx, 2) + bb

    def first_stage(step):
        for i in range(4):
            dx = (i + 2) % 4
            xx = wrap(x + dx, 4)

            def fill_a(u):
                pa[step, xx, u] = acc[tab[96 + row_block(xx, u, 0)]].astype(BF16)

            for u in range(Y):
                fill_a(u)
            if dx:
                rcopy(pa.at[step, xx], ra.at[step, dx - 1], a1s.at[step, dx - 1], a1r.at[step, dx - 1], at_x(xx)).start()
            if i < Y:
                dy = (i + Y // 2) % Y
                yy = wrap(y + dy, Y)

                def fill_b(u):
                    pb[step, yy, u] = acc[tab[96 + row_block(u, yy, 1)]].astype(BF16)

                for u in range(4):
                    fill_b(u)
                if dy:
                    rcopy(pb.at[step, yy], rb.at[step, dy - 1], b1s.at[step, dy - 1], b1r.at[step, dy - 1], at_y(yy)).start()

    def second_stage(step):
        for d in range(3):
            drain(ra.at[step, d], a1r.at[step, d])
        for dy in [Y // 2] + [d for d in range(1, Y) if d != Y // 2] + [0]:
            yy = wrap(y + dy, Y)
            total = pa[step, x, yy].astype(F32)
            for d in range(3):
                total += ra[step, d, yy].astype(F32)
            qa[step, yy] = total.astype(BF16)
            if dy:
                rcopy(qa.at[step, yy], sa.at[step, dy - 1], a2s.at[step, dy - 1], a2r.at[step, dy - 1], at_y(yy)).start()
        for d in range(Y - 1):
            drain(rb.at[step, d], b1r.at[step, d])
        for dx in (2, 1, 3, 0):
            xx = wrap(x + dx, 4)
            total = pb[step, y, xx].astype(F32)
            for d in range(Y - 1):
                total += rb[step, d, xx].astype(F32)
            qb[step, xx] = total.astype(BF16)
            if dx:
                rcopy(qb.at[step, xx], sb.at[step, dx - 1], b2s.at[step, dx - 1], b2r.at[step, dx - 1], at_x(xx)).start()

    def far_first(i):
        return Z // 2 + (1 - 2 * lax.rem(i, 2)) * lax.div(i + 1, 2)

    def third_stage(step):
        for d in range(Y - 1):
            drain(sa.at[step, d], a2r.at[step, d])
        first = qa[step, y].astype(F32)
        for d in range(Y - 1):
            first += sa[step, d].astype(F32)
        for d in range(3):
            drain(sb.at[step, d], b2r.at[step, d])
        second = qb[step, x].astype(F32)
        for d in range(3):
            second += sb[step, d].astype(F32)
        both = jnp.concatenate([first.reshape(Z, zi, 128), second.reshape(Z, zi, 128)], axis=1)
        zs[step] = both.astype(BF16)

        def give(i):
            other = wrap(z + far_first(i), Z)
            rcopy(zs.at[step, other], zr.at[step, z], zss.at[step], zrs.at[step], (other * 2 + xh, s, h)).start()

        loop(Z - 1, give)

    def field(step):
        drain(zr.at[step, pl.ds(0, Z - 1)], zrs.at[step])
        zr[step, z] = zs[step, z]
        return jnp.sum(zr[step].astype(F32), axis=0)

    def gather(step, total):
        incident = jnp.concatenate([ev[step, 0].astype(F32), ev[step, 1].astype(F32)], axis=0)
        dv[step, xh * Z + z] = (incident - total).astype(BF16)
        here = dv.at[step, xh * Z + z]

        if step == 0:
            def give(i):
                other = wrap(z + far_first(i), Z)
                for half in (1 - xh, xh):
                    rcopy(here, here, gss.at[step], grs.at[step], (other * 2 + half, s, h)).start()

            loop(Z - 1, give)
            rcopy(here, here, gss.at[step], grs.at[step], (z * 2 + (1 - xh), s, h)).start()
        else:
            rcopy(here, here, gss.at[step], grs.at[step], (z * 2 + (1 - xh), s, h)).start()

            def hand(i):
                other = i + (z <= i).astype(jnp.int32)
                for half in (1 - xh, xh):
                    rcopy(here, here, gss.at[step], grs.at[step], (other * 2 + half, s, h)).start()

            loop(Z - 1, hand)

    def driven(step):
        drain(dv.at[step, pl.ds(0, K - 1)], grs.at[step])
        for half in range(2):
            chunk = dv[step, half * Z:(half + 1) * Z].astype(F32)
            for bb in range(2):
                dr[step, 2 * half + bb] = chunk[:, bb * zi:(bb + 1) * zi, :].reshape(128, 128).astype(BF16)
        pltpu.make_async_copy(dr.at[step], out.at[step], os.at[step]).start()

    first_stage(0)

    @pl.when(k == 0)
    def _():
        def pack(c):
            pk[:, c] = bv[c].astype(F32).reshape(Z, zi, 128).astype(BF16)

        loop(32, pack)

    def scatter(near, far):
        @pl.when(k == 0)
        def _():
            if near == 0:
                pltpu.make_async_copy(pk.at[0], sl.at[h], cr.at[0]).start()
                pltpu.make_async_copy(key, kv.at[h], cr.at[1]).start()
            for d in range(near + 1, far + 1):
                for other in sorted({d, Z - d}):
                    there = (other * 2 + 0, s, h)
                    rcopy(pk.at[other], sl.at[h], cs.at[0], cr.at[0], there).start()
                    rcopy(key, kv.at[h], cs.at[1], cr.at[1], there).start()

    scatter(0, 1)
    for turn in range(turns):
        heard(turn)
        if turn + 1 < turns:
            tell(turn + 1)
        scatter(1 << turn, 2 << turn)

    @pl.when(k > 0)
    def _():
        drain(x1.at[mine], hr.at[0])
        rcopy(x1.at[mine], x1.at[mine], hs.at[1], hr.at[1], (k, s, 1 - h)).start()

    second_stage(0)

    @pl.when(k > 0)
    def _():
        drain(x1.at[pl.ds(4 - 4 * h, 4)], hr.at[1])
        products(x1)

    @pl.when(k == 0)
    def _():
        def clear(c):
            acc[c] = jnp.zeros((128, 128), F32)

        loop(32, clear)

    third_stage(0)
    first_stage(1)
    gather(0, field(0))

    @pl.when(xh == 0)
    def _():
        drain(sl.at[h], cr.at[0])
        drain(kv.at[h], cr.at[1])
        rcopy(sl.at[h], sl.at[h], cs.at[2], cr.at[0], (k + 1 - 2 * xh, s, h)).start()
        rcopy(kv.at[h], kv.at[h], cs.at[3], cr.at[1], (k + 1 - 2 * xh, s, h)).start()

    second_stage(1)

    @pl.when(xh != 0)
    def _():
        drain(sl.at[h], cr.at[0])
        drain(kv.at[h], cr.at[1])

    rcopy(sl.at[h], sl.at[h], cs.at[4], cr.at[2], (k, s, 1 - h)).start()
    rcopy(kv.at[h], kv.at[h], cs.at[5], cr.at[3], (k, s, 1 - h)).start()
    third_stage(1)

    drain(sl.at[1 - h], cr.at[2])
    drain(kv.at[1 - h], cr.at[3])
    rows, wide = S * 2 * zi, 32 * zi
    m = lax.broadcasted_iota(jnp.int32, (rows, wide), 0)
    n = lax.broadcasted_iota(jnp.int32, (rows, wide), 1)
    q = m // zi
    place = (4 * (q // 2) + 2 * xh + q % 2) * 8 + 4 * h
    same = (m % zi) == (n % zi)
    for half in range(2):
        slots = sl[half].astype(F32).reshape(wide, 128).astype(BF16)
        where = jnp.broadcast_to(kv[half, 0:1, :], (rows, wide))
        for jj in range(4):
            pick = jnp.where(same & (where == place + jj), 1.0, 0.0).astype(BF16)
            ad[half, :, jj * 128:(jj + 1) * 128] = jnp.dot(pick, slots, preferred_element_type=F32).astype(BF16)

    driven(0)
    for b in range(4):
        ov[b * 128:(b + 1) * 128] = jnp.dot(iv[b], dr[0, b], preferred_element_type=F32).astype(BF16)
    newest = ov[...]
    for half in range(2):
        made = jnp.dot(ad[half], newest, preferred_element_type=F32).astype(BF16)
        for other in range(S):
            us[other * 2 + half] = made[other * 2 * zi:(other + 1) * 2 * zi]

    for d in list(range(S, 2 * S)) + list(range(1, S)):
        other = wrap(e + d, 2 * S)
        rcopy(us.at[other], ur.at[e], uss.at[0], urs.at[0], (k, lax.div(other, 2), lax.rem(other, 2))).start()

    rest = field(1)
    drain(ur.at[pl.ds(0, 2 * S - 1)], urs.at[0])
    ur[e] = us[e]
    gather(1, rest + jnp.sum(ur[...].astype(F32), axis=0))
    for step in range(2):
        for d in range(3):
            drain(pa.at[step, 0], a1s.at[step, d])
            drain(qb.at[step, 0], b2s.at[step, d])
        for d in range(Y - 1):
            drain(pb.at[step, 0], b1s.at[step, d])
            drain(qa.at[step, 0], a2s.at[step, d])
        drain(zs.at[step, pl.ds(0, Z - 1)], zss.at[step])
    drain(us.at[pl.ds(0, 2 * S - 1)], uss.at[0])

    @pl.when(k < K - 1)
    def _():
        drain(x1.at[mine], hs.at[0])

    @pl.when(k > 0)
    def _():
        drain(x1.at[mine], hs.at[1])

    @pl.when(k == 0)
    def _():
        drain(bv.at[pl.ds(0, 32 - 32 // Z)], cs.at[0])
        drain(dv.at[0, pl.ds(0, 2 * Z - 2)], cs.at[1])

    @pl.when(xh == 0)
    def _():
        drain(sl.at[h], cs.at[2])
        drain(kv.at[h], cs.at[3])

    drain(sl.at[h], cs.at[4])
    drain(kv.at[h], cs.at[5])
    drain(dv.at[0, pl.ds(0, K - 1)], gss.at[0])
    driven(1)
    drain(dv.at[1, pl.ds(0, K - 1)], gss.at[1])

    for step in range(2):
        pltpu.make_async_copy(dr.at[step], out.at[step], os.at[step]).wait()


def pin(array):
    return pltpu.with_memory_space_constraint(array, pltpu.HBM)


def shards(K, S, blocks, coords, counts, history, excitation, inverse):
    Y, Z = S // 2, K // 2
    zi = 128 // Z
    slots = lax.iota(jnp.int32, 32)
    places = coords[0, 0, 0]
    key = jnp.where(slots < counts[0, 0, 0], places[:, 0] * 8 + places[:, 1], 1 << 20)
    ahead = (key[None, :] < key[:, None]) | ((key[None, :] == key[:, None]) & (slots[None, :] < slots[:, None]))
    rank = jnp.sum(ahead.astype(jnp.int32), axis=1)
    chosen = rank[None, :] == slots[:, None]
    order = jnp.sum(jnp.where(chosen, slots[None, :], 0), axis=1)
    placed = jnp.sum(jnp.where(chosen, key[None, :], 0), axis=1)
    row = placed // 8
    before = jnp.sum(jnp.where(rank[None, :] == slots[:, None] - 1, key[None, :] // 8, 0), axis=1)
    keep = ((slots > 0) & (row == before)).astype(jnp.int32)
    last = jnp.max(jnp.where(key[None, :] // 8 == lax.iota(jnp.int32, 4 * S)[:, None], rank[None, :], -1), axis=1)
    last = jnp.where(last < 0, 32, last)
    tab = jnp.concatenate([order, placed % 8, keep, last])
    wide = jnp.broadcast_to(key[None, :, None], (8, 32, zi)).reshape(8, 32 * zi)
    dma = pltpu.SemaphoreType.DMA
    v = pltpu.VMEM
    scratch = [
        v((32, 128, 128), BF16), v((Z, 32, zi, 128), BF16), v((8, 128, 128), BF16), v((8, 128, 128), BF16), v((2, 2, zi, 128), BF16), v((4, 128, 128), BF16),
        v((33, 128, 128), F32), v((2, 4, 128, 128), BF16),
        v((2, 4, Y, 128, 128), BF16), v((2, Y, 4, 128, 128), BF16),
        v((2, 3, Y, 128, 128), BF16), v((2, Y - 1, 4, 128, 128), BF16),
        v((2, Y, 128, 128), BF16), v((2, 4, 128, 128), BF16),
        v((2, Y - 1, 128, 128), BF16), v((2, 3, 128, 128), BF16),
        v((2, Z, 2 * zi, 128), BF16), v((2, Z, 2 * zi, 128), BF16), v((2, K, 2 * zi, 128), BF16),
        v((2, 32, zi, 128), BF16), v((2, 8, 32 * zi), jnp.int32), v((2, S * 2 * zi, 512), BF16),
        v((2 * S, 2 * zi, 128), BF16), v((2 * S, 2 * zi, 128), BF16), v((512, 128), BF16),
        dma((7,)), dma((2, 3)), dma((2, 3)), dma((2, Y - 1)), dma((2, Y - 1)),
        dma((2, Y - 1)), dma((2, Y - 1)), dma((2, 3)), dma((2, 3)),
        dma((2,)), dma((2,)), dma((2,)), dma((2,)), dma((1,)), dma((1,)), dma((2,)), dma((2,)), dma((6,)), dma((4,)), dma((2,)),
        pltpu.SemaphoreType.REGULAR((4,)),
    ]
    hbm = pl.BlockSpec(memory_space=pltpu.HBM)
    made = pl.pallas_call(
        functools.partial(kernel, K, Y),
        out_shape=jax.ShapeDtypeStruct((2, 4, 128, 128), BF16),
        in_specs=[pl.BlockSpec(memory_space=pltpu.SMEM), pl.BlockSpec(memory_space=pl.ANY)] + [hbm] * 4,
        out_specs=pl.BlockSpec(memory_space=pl.ANY),
        scratch_shapes=scratch,
        compiler_params=pltpu.CompilerParams(
            collective_id=0, has_side_effects=True, vmem_limit_bytes=40 * 1024 * 1024),
        name="march",
    )(
        tab, wide, pin(blocks[0, 0, 0]), pin(history[0].reshape(8, 128, 128)),
        pin(excitation[:, 0].reshape(2, 4, 128, 128)), pin(inverse[0]),
    )
    both = jnp.broadcast_to(inverse[0][None], made.shape)
    currents = jnp.einsum("nbij,nbjw->nbiw", both, made, preferred_element_type=F32)
    return currents.astype(BF16).reshape(2, 1, 512, 128)


def solution(mesh):
    placed = (
        P("delay", "src", "tgt", None, None, None),
        P("delay", "src", "tgt", None, None),
        P("delay", "src", "tgt"),
        P("delay", None, "src", None),
        P(None, "tgt", "src", None),
        P("tgt", "src", None, None),
    )
    return jax.shard_map(
        functools.partial(shards, mesh.shape["delay"], mesh.shape["src"]),
        mesh=mesh, in_specs=placed, out_specs=P(None, "tgt", "src", None), check_vma=False,
    )
```

```python
import functools

import jax
import jax.numpy as jnp
from jax import lax
from jax.experimental import pallas as pl
from jax.experimental.pallas import tpu as pltpu
from jax.sharding import PartitionSpec as P

MESH = pl.DeviceIdType.MESH
F32 = jnp.float32
BF16 = jnp.bfloat16


def rcopy(src, dst, send, recv, device):
    return pltpu.make_async_remote_copy(
        src_ref=src, dst_ref=dst, send_sem=send, recv_sem=recv, device_id=device, device_id_type=MESH
    )


def drain(ref, sem):
    pltpu.make_async_copy(ref, ref, sem).wait()


def inside(value, size):
    return jnp.minimum(jnp.maximum(value, 0), size - 1)


def wrap(value, size):
    return lax.rem(value, size)


def loop(count, body):
    def step(i, carry):
        body(i)
        return carry

    lax.fori_loop(0, count, step, 0)


def kernel(
    K, Y,
    places, used, blocks, hist, exc, inv, out,
    cv, tv, tab, key, bv, pk, x0, x1, ev, iv, acc, dr, pa, pb, ra, rb, qa, qb, sa, sb, zs, zr, dv, sl, kv, ad, us, ur, ov,
    ld, a1s, a1r, b1s, b1r, a2s, a2r, b2s, b2r, zss, zrs, gss, grs, uss, urs, hs, hr, cs, cr, os, known,
):
    k, s, h = lax.axis_index("delay"), lax.axis_index("src"), lax.axis_index("tgt")
    Z = K // 2
    S = 2 * Y
    zi = 128 // Z
    z, xh = lax.div(k, 2), lax.rem(k, 2)
    xl, y = lax.div(s, Y), lax.rem(s, Y)
    x = xh * 2 + xl
    e = s * 2 + h

    def at_x(other):
        return (z * 2 + lax.div(other, 2), lax.rem(other, 2) * Y + y, h)

    def at_y(other):
        return (k, xl * Y + other, h)

    small = [
        pltpu.make_async_copy(places, cv, ld.at[7]),
    ]
    loads = [
        pltpu.make_async_copy(blocks, bv, ld.at[0]),
        pltpu.make_async_copy(hist, x0, ld.at[1]),
        pltpu.make_async_copy(inv, iv, ld.at[2]),
    ]
    for step in range(2):
        for bb in range(2):
            loads.append(pltpu.make_async_copy(
                exc.at[step, 2 * xh + bb, pl.ds(z * zi, zi)], ev.at[step, bb], ld.at[3 + step * 2 + bb]))
    for copy in small + loads:
        copy.start()

    barrier = pltpu.get_barrier_semaphore()

    def greet(device):
        pl.semaphore_signal(barrier, inc=1, device_id=device, device_id_type=MESH)

    for d in range(1, 2 * S):
        other = wrap(e + d, 2 * S)
        greet((k, lax.div(other, 2), lax.rem(other, 2)))
    greet((k + 1 - 2 * xh, s, h))
    greet(at_x(3 - x))
    greet((wrap(k + 2 * xh - 1 + K, K), s, h))
    greet((wrap(k + 2, K), s, h))
    greet((wrap(k + K - 2, K), s, h))

    for copy in small:
        copy.wait()
    shape = (32, 32)
    sub = lax.broadcasted_iota(jnp.int32, shape, 0)
    lane = lax.broadcasted_iota(jnp.int32, shape, 1)
    spot = cv[0:1, :] * 8 + cv[1:2, :]
    along = jnp.where(lane < used[0], jnp.broadcast_to(spot, shape), 1024)
    down = jnp.broadcast_to(jnp.sum(jnp.where(sub == lane, along, 0), axis=1, keepdims=True), shape)
    ahead = (along < down) | ((along == down) & (lane < sub))
    rank = jnp.broadcast_to(jnp.sum(jnp.where(ahead, 1, 0), axis=1, keepdims=True), shape)
    row = lax.div(down, 8)
    chosen = rank == lane

    def column_sum(mask, value):
        return jnp.sum(jnp.where(mask, value, 0), axis=0, keepdims=True)

    order = column_sum(chosen, sub)
    column = column_sum(chosen, down - row * 8)
    here = column_sum(chosen, row)
    before = column_sum(rank == lane - 1, row + 1) - 1
    keep = jnp.where(here == before, 1, 0)
    last = jnp.max(jnp.where(row == lane, rank, -1), axis=0, keepdims=True)
    last = jnp.where(last < 0, 32, last)
    tv[...] = jnp.zeros((8, 128), jnp.int32)
    for i, value in enumerate((order, column, keep, last)):
        tv[i:i + 1, 0:32] = value
    key[...] = jnp.full((8, 128), -1.0, F32)
    key[0:1, 0:32] = along[0:1, :].astype(F32)
    listed = pltpu.make_async_copy(tv, tab, ld.at[9])
    listed.start()
    acc[32] = jnp.zeros((128, 128), F32)
    listed.wait()

    def products(tile):
        def body(g):
            total = acc[wrap(4 * g + 32, 33)]
            for c in range(4):
                c = 4 * g + c
                made = jnp.dot(bv[inside(tab[0, c], 32)], tile[inside(tab[1, c], 8)], preferred_element_type=F32)
                total = made + total * tab[2, c].astype(F32)
                acc[c] = total

        loop(8, body)


    loads[0].wait()
    loads[1].wait()
    products(x0)
    pl.semaphore_wait(barrier, (2 * S - 1) + 5)

    def tell(turn):
        for d in (1 << turn, Z - (1 << turn)):
            pl.semaphore_signal(known.at[turn], inc=1, device_id=(wrap(z + d, Z) * 2 + xh, s, h), device_id_type=MESH)

    def heard(turn):
        pl.semaphore_wait(known.at[turn], 2)

    turns = max(Z // 2, 1).bit_length() - 1
    if turns > 0:
        tell(0)

    mine = pl.ds(4 * h, 4)

    @pl.when(k < K - 1)
    def _():
        rcopy(hist.at[mine], x1.at[mine], hs.at[0], hr.at[0], (k + 1, s, h)).start()

    for copy in loads[2:]:
        copy.wait()

    def row_block(xx, yy, bb):
        return 4 * (lax.rem(xx, 2) * Y + yy) + 2 * lax.div(xx, 2) + bb

    def first_stage(step):
        for i in range(4):
            dx = (i + 2) % 4
            xx = wrap(x + dx, 4)

            def fill_a(u):
                pa[step, xx, u] = acc[inside(tab[3, row_block(xx, u, 0)], 33)].astype(BF16)

            for u in range(Y):
                fill_a(u)
            if dx:
                rcopy(pa.at[step, xx], ra.at[step, dx - 1], a1s.at[step, dx - 1], a1r.at[step, dx - 1], at_x(xx)).start()
            if i < Y:
                dy = (i + Y // 2) % Y
                yy = wrap(y + dy, Y)

                def fill_b(u):
                    pb[step, yy, u] = acc[inside(tab[3, row_block(u, yy, 1)], 33)].astype(BF16)

                for u in range(4):
                    fill_b(u)
                if dy:
                    rcopy(pb.at[step, yy], rb.at[step, dy - 1], b1s.at[step, dy - 1], b1r.at[step, dy - 1], at_y(yy)).start()

    def second_stage(step):
        for d in range(3):
            drain(ra.at[step, d], a1r.at[step, d])
        for dy in [Y // 2] + [d for d in range(1, Y) if d != Y // 2] + [0]:
            yy = wrap(y + dy, Y)
            total = pa[step, x, yy].astype(F32)
            for d in range(3):
                total += ra[step, d, yy].astype(F32)
            qa[step, yy] = total.astype(BF16)
            if dy:
                rcopy(qa.at[step, yy], sa.at[step, dy - 1], a2s.at[step, dy - 1], a2r.at[step, dy - 1], at_y(yy)).start()
        for d in range(Y - 1):
            drain(rb.at[step, d], b1r.at[step, d])
        for dx in (2, 1, 3, 0):
            xx = wrap(x + dx, 4)
            total = pb[step, y, xx].astype(F32)
            for d in range(Y - 1):
                total += rb[step, d, xx].astype(F32)
            qb[step, xx] = total.astype(BF16)
            if dx:
                rcopy(qb.at[step, xx], sb.at[step, dx - 1], b2s.at[step, dx - 1], b2r.at[step, dx - 1], at_x(xx)).start()

    def far_first(i):
        return Z // 2 + (1 - 2 * lax.rem(i, 2)) * lax.div(i + 1, 2)

    def third_stage(step):
        for d in range(Y - 1):
            drain(sa.at[step, d], a2r.at[step, d])
        first = qa[step, y].astype(F32)
        for d in range(Y - 1):
            first += sa[step, d].astype(F32)
        for d in range(3):
            drain(sb.at[step, d], b2r.at[step, d])
        second = qb[step, x].astype(F32)
        for d in range(3):
            second += sb[step, d].astype(F32)
        both = jnp.concatenate([first.reshape(Z, zi, 128), second.reshape(Z, zi, 128)], axis=1)
        zs[step] = both.astype(BF16)

        def give(i):
            other = wrap(z + far_first(i), Z)
            rcopy(zs.at[step, other], zr.at[step, z], zss.at[step], zrs.at[step], (other * 2 + xh, s, h)).start()

        loop(Z - 1, give)

    def field(step):
        drain(zr.at[step, pl.ds(0, Z - 1)], zrs.at[step])
        zr[step, z] = zs[step, z]
        return jnp.sum(zr[step].astype(F32), axis=0)

    def gather(step, total):
        incident = jnp.concatenate([ev[step, 0].astype(F32), ev[step, 1].astype(F32)], axis=0)
        dv[step, xh * Z + z] = (incident - total).astype(BF16)
        here = dv.at[step, xh * Z + z]

        if step == 0:
            def give(i):
                other = wrap(z + far_first(i), Z)
                for half in (1 - xh, xh):
                    rcopy(here, here, gss.at[step], grs.at[step], (other * 2 + half, s, h)).start()

            loop(Z - 1, give)
            rcopy(here, here, gss.at[step], grs.at[step], (z * 2 + (1 - xh), s, h)).start()
        else:
            rcopy(here, here, gss.at[step], grs.at[step], (z * 2 + (1 - xh), s, h)).start()

            def hand(i):
                other = i + (z <= i).astype(jnp.int32)
                for half in (1 - xh, xh):
                    rcopy(here, here, gss.at[step], grs.at[step], (other * 2 + half, s, h)).start()

            loop(Z - 1, hand)

    def driven(step):
        drain(dv.at[step, pl.ds(0, K - 1)], grs.at[step])
        for half in range(2):
            chunk = dv[step, half * Z:(half + 1) * Z].astype(F32)
            for bb in range(2):
                dr[step, 2 * half + bb] = chunk[:, bb * zi:(bb + 1) * zi, :].reshape(128, 128).astype(BF16)
        pltpu.make_async_copy(dr.at[step], out.at[step], os.at[step]).start()

    first_stage(0)

    @pl.when(k == 0)
    def _():
        def pack(c):
            pk[:, c] = bv[c].astype(F32).reshape(Z, zi, 128).astype(BF16)

        loop(32, pack)

    def scatter(near, far):
        @pl.when(k == 0)
        def _():
            if near == 0:
                pltpu.make_async_copy(pk.at[0], sl.at[h], cr.at[0]).start()
                pltpu.make_async_copy(key, kv.at[h], cr.at[1]).start()
            for d in range(near + 1, far + 1):
                for other in sorted({d, Z - d}):
                    there = (other * 2 + 0, s, h)
                    rcopy(pk.at[other], sl.at[h], cs.at[0], cr.at[0], there).start()
                    rcopy(key, kv.at[h], cs.at[1], cr.at[1], there).start()

    scatter(0, 1)
    for turn in range(turns):
        heard(turn)
        if turn + 1 < turns:
            tell(turn + 1)
        scatter(1 << turn, 2 << turn)

    @pl.when(k > 0)
    def _():
        drain(x1.at[mine], hr.at[0])
        rcopy(x1.at[mine], x1.at[mine], hs.at[1], hr.at[1], (k, s, 1 - h)).start()

    second_stage(0)

    @pl.when(k > 0)
    def _():
        drain(x1.at[pl.ds(4 - 4 * h, 4)], hr.at[1])
        products(x1)

    @pl.when(k == 0)
    def _():
        def clear(c):
            acc[c] = jnp.zeros((128, 128), F32)

        loop(32, clear)

    third_stage(0)
    first_stage(1)
    gather(0, field(0))

    @pl.when(xh == 0)
    def _():
        drain(sl.at[h], cr.at[0])
        drain(kv.at[h], cr.at[1])
        rcopy(sl.at[h], sl.at[h], cs.at[2], cr.at[0], (k + 1 - 2 * xh, s, h)).start()
        rcopy(kv.at[h], kv.at[h], cs.at[3], cr.at[1], (k + 1 - 2 * xh, s, h)).start()

    second_stage(1)

    @pl.when(xh != 0)
    def _():
        drain(sl.at[h], cr.at[0])
        drain(kv.at[h], cr.at[1])

    rcopy(sl.at[h], sl.at[h], cs.at[4], cr.at[2], (k, s, 1 - h)).start()
    rcopy(kv.at[h], kv.at[h], cs.at[5], cr.at[3], (k, s, 1 - h)).start()
    third_stage(1)

    drain(sl.at[1 - h], cr.at[2])
    drain(kv.at[1 - h], cr.at[3])
    rows, wide = S * 2 * zi, 32 * zi
    m = lax.broadcasted_iota(jnp.int32, (rows, wide), 0)
    n = lax.broadcasted_iota(jnp.int32, (rows, wide), 1)
    q = m // zi
    place = (4 * (q // 2) + 2 * xh + q % 2) * 8 + 4 * h
    same = (m % zi) == (n % zi)
    spread = jnp.where(
        lax.broadcasted_iota(jnp.int32, (128, wide), 0) == lax.broadcasted_iota(jnp.int32, (128, wide), 1) // zi, 1.0, 0.0).astype(BF16)
    place = place.astype(F32)
    for half in range(2):
        slots = sl[half].astype(F32).reshape(wide, 128).astype(BF16)
        named = jnp.dot(kv[half].astype(BF16), spread, preferred_element_type=F32)
        where = jnp.broadcast_to(named[0:1, :], (rows, wide))
        for jj in range(4):
            pick = jnp.where(same & (where == place + float(jj)), 1.0, 0.0).astype(BF16)
            ad[half, :, jj * 128:(jj + 1) * 128] = jnp.dot(pick, slots, preferred_element_type=F32).astype(BF16)

    driven(0)
    for b in range(4):
        ov[b * 128:(b + 1) * 128] = jnp.dot(iv[b], dr[0, b], preferred_element_type=F32).astype(BF16)
    newest = ov[...]
    for half in range(2):
        made = jnp.dot(ad[half], newest, preferred_element_type=F32).astype(BF16)
        for other in range(S):
            us[other * 2 + half] = made[other * 2 * zi:(other + 1) * 2 * zi]

    for d in list(range(S, 2 * S)) + list(range(1, S)):
        other = wrap(e + d, 2 * S)
        rcopy(us.at[other], ur.at[e], uss.at[0], urs.at[0], (k, lax.div(other, 2), lax.rem(other, 2))).start()

    rest = field(1)
    drain(ur.at[pl.ds(0, 2 * S - 1)], urs.at[0])
    ur[e] = us[e]
    gather(1, rest + jnp.sum(ur[...].astype(F32), axis=0))
    for step in range(2):
        for d in range(3):
            drain(pa.at[step, 0], a1s.at[step, d])
            drain(qb.at[step, 0], b2s.at[step, d])
        for d in range(Y - 1):
            drain(pb.at[step, 0], b1s.at[step, d])
            drain(qa.at[step, 0], a2s.at[step, d])
        drain(zs.at[step, pl.ds(0, Z - 1)], zss.at[step])
    drain(us.at[pl.ds(0, 2 * S - 1)], uss.at[0])

    @pl.when(k < K - 1)
    def _():
        drain(x1.at[mine], hs.at[0])

    @pl.when(k > 0)
    def _():
        drain(x1.at[mine], hs.at[1])

    @pl.when(k == 0)
    def _():
        drain(bv.at[pl.ds(0, 32 - 32 // Z)], cs.at[0])
        drain(acc.at[0, pl.ds(0, 8 * (Z - 1))], cs.at[1])

    @pl.when(xh == 0)
    def _():
        drain(sl.at[h], cs.at[2])
        drain(kv.at[h], cs.at[3])

    drain(sl.at[h], cs.at[4])
    drain(kv.at[h], cs.at[5])
    drain(dv.at[0, pl.ds(0, K - 1)], gss.at[0])
    driven(1)
    drain(dv.at[1, pl.ds(0, K - 1)], gss.at[1])

    for step in range(2):
        pltpu.make_async_copy(dr.at[step], out.at[step], os.at[step]).wait()


def pin(array):
    return pltpu.with_memory_space_constraint(array, pltpu.HBM)


def shards(K, S, blocks, coords, counts, history, excitation, inverse):
    Y, Z = S // 2, K // 2
    zi = 128 // Z
    dma = pltpu.SemaphoreType.DMA
    v = pltpu.VMEM
    scratch = [
        v((2, 32), jnp.int32), v((8, 128), jnp.int32), pltpu.SMEM((8, 128), jnp.int32), v((8, 128), F32),
        v((32, 128, 128), BF16), v((Z, 32, zi, 128), BF16), v((8, 128, 128), BF16), v((8, 128, 128), BF16), v((2, 2, zi, 128), BF16), v((4, 128, 128), BF16),
        v((33, 128, 128), F32), v((2, 4, 128, 128), BF16),
        v((2, 4, Y, 128, 128), BF16), v((2, Y, 4, 128, 128), BF16),
        v((2, 3, Y, 128, 128), BF16), v((2, Y - 1, 4, 128, 128), BF16),
        v((2, Y, 128, 128), BF16), v((2, 4, 128, 128), BF16),
        v((2, Y - 1, 128, 128), BF16), v((2, 3, 128, 128), BF16),
        v((2, Z, 2 * zi, 128), BF16), v((2, Z, 2 * zi, 128), BF16), v((2, K, 2 * zi, 128), BF16),
        v((2, 32, zi, 128), BF16), v((2, 8, 128), F32), v((2, S * 2 * zi, 512), BF16),
        v((2 * S, 2 * zi, 128), BF16), v((2 * S, 2 * zi, 128), BF16), v((512, 128), BF16),
        dma((10,)), dma((2, 3)), dma((2, 3)), dma((2, Y - 1)), dma((2, Y - 1)),
        dma((2, Y - 1)), dma((2, Y - 1)), dma((2, 3)), dma((2, 3)),
        dma((2,)), dma((2,)), dma((2,)), dma((2,)), dma((1,)), dma((1,)), dma((2,)), dma((2,)), dma((6,)), dma((4,)), dma((2,)),
        pltpu.SemaphoreType.REGULAR((4,)),
    ]
    hbm = pl.BlockSpec(memory_space=pltpu.HBM)
    made = pl.pallas_call(
        functools.partial(kernel, K, Y),
        out_shape=jax.ShapeDtypeStruct((2, 4, 128, 128), BF16),
        in_specs=[hbm, pl.BlockSpec(memory_space=pltpu.SMEM)] + [hbm] * 4,
        out_specs=pl.BlockSpec(memory_space=pl.ANY),
        scratch_shapes=scratch,
        compiler_params=pltpu.CompilerParams(
            collective_id=0, has_side_effects=True, vmem_limit_bytes=40 * 1024 * 1024),
        name="march",
    )(
        pin(coords[0, 0, 0].T), counts[0, 0], pin(blocks[0, 0, 0]), pin(history[0].reshape(8, 128, 128)),
        pin(excitation[:, 0].reshape(2, 4, 128, 128)), pin(inverse[0]),
    )
    both = jnp.broadcast_to(inverse[0][None], made.shape)
    currents = jnp.einsum("nbij,nbjw->nbiw", both, made, preferred_element_type=F32)
    return currents.astype(BF16).reshape(2, 1, 512, 128)


def solution(mesh):
    placed = (
        P("delay", "src", "tgt", None, None, None),
        P("delay", "src", "tgt", None, None),
        P("delay", "src", "tgt"),
        P("delay", None, "src", None),
        P(None, "tgt", "src", None),
        P("tgt", "src", None, None),
    )
    return jax.shard_map(
        functools.partial(shards, mesh.shape["delay"], mesh.shape["src"]),
        mesh=mesh, in_specs=placed, out_specs=P(None, "tgt", "src", None), check_vma=False,
    )
```

```python
import functools

import jax
import jax.numpy as jnp
from jax import lax
from jax.experimental import pallas as pl
from jax.experimental.pallas import tpu as pltpu
from jax.sharding import PartitionSpec as P

MESH = pl.DeviceIdType.MESH
F32 = jnp.float32
BF16 = jnp.bfloat16


def rcopy(src, dst, send, recv, device):
    return pltpu.make_async_remote_copy(
        src_ref=src, dst_ref=dst, send_sem=send, recv_sem=recv, device_id=device, device_id_type=MESH
    )


def drain(ref, sem):
    pltpu.make_async_copy(ref, ref, sem).wait()


def inside(value, size):
    return jnp.minimum(jnp.maximum(value, 0), size - 1)


def wrap(value, size):
    return lax.rem(value, size)


def loop(count, body):
    def step(i, carry):
        body(i)
        return carry

    lax.fori_loop(0, count, step, 0)


def kernel(
    K, Y,
    places, used, blocks, hist, exc, inv, out,
    cv, tv, tab, key, bv, pk, x0, x1, ev, iv, acc, dr, pa, pb, ra, rb, qa, qb, sa, sb, zs, zr, dv, sl, kv, ad, us, ur, ov,
    ld, a1s, a1r, b1s, b1r, a2s, a2r, b2s, b2r, zss, zrs, gss, grs, uss, urs, hs, hr, cs, cr, os, known,
):
    k, s, h = lax.axis_index("delay"), lax.axis_index("src"), lax.axis_index("tgt")
    Z = K // 2
    S = 2 * Y
    zi = 128 // Z
    z, xh = lax.div(k, 2), lax.rem(k, 2)
    xl, y = lax.div(s, Y), lax.rem(s, Y)
    x = xh * 2 + xl
    e = s * 2 + h

    def at_x(other):
        return (z * 2 + lax.div(other, 2), lax.rem(other, 2) * Y + y, h)

    def at_y(other):
        return (k, xl * Y + other, h)

    small = [
        pltpu.make_async_copy(places, cv, ld.at[7]),
    ]
    loads = [
        pltpu.make_async_copy(blocks, bv, ld.at[0]),
        pltpu.make_async_copy(hist, x0, ld.at[1]),
        pltpu.make_async_copy(inv, iv, ld.at[2]),
    ]
    for step in range(2):
        for bb in range(2):
            loads.append(pltpu.make_async_copy(
                exc.at[step, 2 * xh + bb, pl.ds(z * zi, zi)], ev.at[step, bb], ld.at[3 + step * 2 + bb]))
    for copy in small + loads:
        copy.start()

    barrier = pltpu.get_barrier_semaphore()

    def greet(device):
        pl.semaphore_signal(barrier, inc=1, device_id=device, device_id_type=MESH)

    for d in range(1, 2 * S):
        other = wrap(e + d, 2 * S)
        greet((k, lax.div(other, 2), lax.rem(other, 2)))
    greet((k + 1 - 2 * xh, s, h))
    greet(at_x(3 - x))
    greet((wrap(k + 2 * xh - 1 + K, K), s, h))
    greet((wrap(k + 2, K), s, h))
    greet((wrap(k + K - 2, K), s, h))

    for copy in small:
        copy.wait()
    shape = (32, 32)
    sub = lax.broadcasted_iota(jnp.int32, shape, 0)
    lane = lax.broadcasted_iota(jnp.int32, shape, 1)
    spot = cv[0:1, :] * 8 + cv[1:2, :]
    along = jnp.where(lane < used[0], jnp.broadcast_to(spot, shape), 1024)
    down = jnp.broadcast_to(jnp.sum(jnp.where(sub == lane, along, 0), axis=1, keepdims=True), shape)
    ahead = (along < down) | ((along == down) & (lane < sub))
    rank = jnp.broadcast_to(jnp.sum(jnp.where(ahead, 1, 0), axis=1, keepdims=True), shape)
    row = lax.div(down, 8)
    chosen = rank == lane

    def column_sum(mask, value):
        return jnp.sum(jnp.where(mask, value, 0), axis=0, keepdims=True)

    order = column_sum(chosen, sub)
    column = column_sum(chosen, down - row * 8)
    here = column_sum(chosen, row)
    before = column_sum(rank == lane - 1, row + 1) - 1
    keep = jnp.where(here == before, 1, 0)
    last = jnp.max(jnp.where(row == lane, rank, -1), axis=0, keepdims=True)
    last = jnp.where(last < 0, 32, last)
    tv[...] = jnp.zeros((8, 128), jnp.int32)
    for i, value in enumerate((order, column, keep, last)):
        tv[i:i + 1, 0:32] = value
    key[...] = jnp.full((8, 128), -1.0, F32)
    key[0:1, 0:32] = along[0:1, :].astype(F32)
    listed = pltpu.make_async_copy(tv, tab, ld.at[9])
    listed.start()
    acc[32] = jnp.zeros((128, 128), F32)
    listed.wait()

    def products(tile):
        def body(g):
            total = acc[wrap(4 * g + 32, 33)]
            for c in range(4):
                c = 4 * g + c
                made = jnp.dot(bv[inside(tab[0, c], 32)], tile[inside(tab[1, c], 8)], preferred_element_type=F32)
                total = made + total * tab[2, c].astype(F32)
                acc[c] = total

        loop(8, body)

    loads[0].wait()
    loads[1].wait()
    products(x0)
    pl.semaphore_wait(barrier, (2 * S - 1) + 5)

    def tell(turn):
        for d in (1 << turn, Z - (1 << turn)):
            pl.semaphore_signal(known.at[turn], inc=1, device_id=(wrap(z + d, Z) * 2 + xh, s, h), device_id_type=MESH)

    def heard(turn):
        pl.semaphore_wait(known.at[turn], 2)

    turns = max(Z // 2, 1).bit_length() - 1
    if turns > 0:
        tell(0)

    mine = pl.ds(4 * h, 4)

    for copy in loads[2:]:
        copy.wait()

    def row_block(xx, yy, bb):
        return 4 * (lax.rem(xx, 2) * Y + yy) + 2 * lax.div(xx, 2) + bb

    def first_stage(step):
        for i in range(4):
            dx = (3, 2, 1, 0)[i]
            xx = wrap(x + dx, 4)

            def fill_a(u):
                pa[step, xx, u] = acc[inside(tab[3, row_block(xx, u, 0)], 33)].astype(BF16)

            for u in range(Y):
                fill_a(u)
            if dx:
                rcopy(pa.at[step, xx], ra.at[step, dx - 1], a1s.at[step, dx - 1], a1r.at[step, dx - 1], at_x(xx)).start()
            if i < Y:
                dy = (Y - 1 - i) % Y
                yy = wrap(y + dy, Y)

                def fill_b(u):
                    pb[step, yy, u] = acc[inside(tab[3, row_block(u, yy, 1)], 33)].astype(BF16)

                for u in range(4):
                    fill_b(u)
                if dy:
                    rcopy(pb.at[step, yy], rb.at[step, dy - 1], b1s.at[step, dy - 1], b1r.at[step, dy - 1], at_y(yy)).start()

    def second_stage(step):
        for d in range(3):
            drain(ra.at[step, d], a1r.at[step, d])
        for dy in [Y // 2] + [d for d in range(1, Y) if d != Y // 2] + [0]:
            yy = wrap(y + dy, Y)
            total = pa[step, x, yy].astype(F32)
            for d in range(3):
                total += ra[step, d, yy].astype(F32)
            qa[step, yy] = total.astype(BF16)
            if dy:
                rcopy(qa.at[step, yy], sa.at[step, dy - 1], a2s.at[step, dy - 1], a2r.at[step, dy - 1], at_y(yy)).start()
        for d in range(Y - 1):
            drain(rb.at[step, d], b1r.at[step, d])
        for dx in (2, 1, 3, 0):
            xx = wrap(x + dx, 4)
            total = pb[step, y, xx].astype(F32)
            for d in range(Y - 1):
                total += rb[step, d, xx].astype(F32)
            qb[step, xx] = total.astype(BF16)
            if dx:
                rcopy(qb.at[step, xx], sb.at[step, dx - 1], b2s.at[step, dx - 1], b2r.at[step, dx - 1], at_x(xx)).start()

    def far_first(i):
        return Z // 2 + (1 - 2 * lax.rem(i, 2)) * lax.div(i + 1, 2)

    def third_stage(step):
        for d in range(Y - 1):
            drain(sa.at[step, d], a2r.at[step, d])
        first = qa[step, y].astype(F32)
        for d in range(Y - 1):
            first += sa[step, d].astype(F32)
        for d in range(3):
            drain(sb.at[step, d], b2r.at[step, d])
        second = qb[step, x].astype(F32)
        for d in range(3):
            second += sb[step, d].astype(F32)
        both = jnp.concatenate([first.reshape(Z, zi, 128), second.reshape(Z, zi, 128)], axis=1)
        zs[step] = both.astype(BF16)

        def give(i):
            other = wrap(z + far_first(i), Z)
            rcopy(zs.at[step, other], zr.at[step, z], zss.at[step], zrs.at[step], (other * 2 + xh, s, h)).start()

        loop(Z - 1, give)

    def field(step):
        drain(zr.at[step, pl.ds(0, Z - 1)], zrs.at[step])
        zr[step, z] = zs[step, z]
        return jnp.sum(zr[step].astype(F32), axis=0)

    def gather(step, total):
        incident = jnp.concatenate([ev[step, 0].astype(F32), ev[step, 1].astype(F32)], axis=0)
        dv[step, xh * Z + z] = (incident - total).astype(BF16)
        here = dv.at[step, xh * Z + z]

        if step == 0:
            def give(i):
                other = wrap(z + far_first(i), Z)
                for half in (1 - xh, xh):
                    rcopy(here, here, gss.at[step], grs.at[step], (other * 2 + half, s, h)).start()

            loop(Z - 1, give)
            rcopy(here, here, gss.at[step], grs.at[step], (z * 2 + (1 - xh), s, h)).start()
        else:
            rcopy(here, here, gss.at[step], grs.at[step], (z * 2 + (1 - xh), s, h)).start()

            def hand(i):
                other = i + (z <= i).astype(jnp.int32)
                for half in (1 - xh, xh):
                    rcopy(here, here, gss.at[step], grs.at[step], (other * 2 + half, s, h)).start()

            loop(Z - 1, hand)

    def driven(step):
        drain(dv.at[step, pl.ds(0, K - 1)], grs.at[step])
        for half in range(2):
            chunk = dv[step, half * Z:(half + 1) * Z].astype(F32)
            for bb in range(2):
                dr[step, 2 * half + bb] = chunk[:, bb * zi:(bb + 1) * zi, :].reshape(128, 128).astype(BF16)
        pltpu.make_async_copy(dr.at[step], out.at[step], os.at[step]).start()

    first_stage(0)

    @pl.when(k < K - 1)
    def _():
        rcopy(hist.at[mine], x1.at[mine], hs.at[0], hr.at[0], (k + 1, s, h)).start()


    @pl.when(k == 0)
    def _():
        def pack(c):
            pk[:, c] = bv[c].astype(F32).reshape(Z, zi, 128).astype(BF16)

        loop(32, pack)

    def scatter(near, far):
        @pl.when(k == 0)
        def _():
            if near == 0:
                pltpu.make_async_copy(pk.at[0], sl.at[h], cr.at[0]).start()
                pltpu.make_async_copy(key, kv.at[h], cr.at[1]).start()
            for d in range(near + 1, far + 1):
                for other in sorted({d, Z - d}):
                    there = (other * 2 + 0, s, h)
                    rcopy(pk.at[other], sl.at[h], cs.at[0], cr.at[0], there).start()
                    rcopy(key, kv.at[h], cs.at[1], cr.at[1], there).start()

    scatter(0, 1)
    for turn in range(turns):
        heard(turn)
        if turn + 1 < turns:
            tell(turn + 1)
        scatter(1 << turn, 2 << turn)

    @pl.when(k > 0)
    def _():
        drain(x1.at[mine], hr.at[0])
        rcopy(x1.at[mine], x1.at[mine], hs.at[1], hr.at[1], (k, s, 1 - h)).start()

    second_stage(0)

    @pl.when(k > 0)
    def _():
        drain(x1.at[pl.ds(4 - 4 * h, 4)], hr.at[1])
        products(x1)

    @pl.when(k == 0)
    def _():
        def clear(c):
            acc[c] = jnp.zeros((128, 128), F32)

        loop(32, clear)

    third_stage(0)
    first_stage(1)
    gather(0, field(0))

    @pl.when(xh == 0)
    def _():
        drain(sl.at[h], cr.at[0])
        drain(kv.at[h], cr.at[1])
        rcopy(sl.at[h], sl.at[h], cs.at[2], cr.at[0], (k + 1 - 2 * xh, s, h)).start()
        rcopy(kv.at[h], kv.at[h], cs.at[3], cr.at[1], (k + 1 - 2 * xh, s, h)).start()

    second_stage(1)

    @pl.when(xh != 0)
    def _():
        drain(sl.at[h], cr.at[0])
        drain(kv.at[h], cr.at[1])

    rcopy(sl.at[h], sl.at[h], cs.at[4], cr.at[2], (k, s, 1 - h)).start()
    rcopy(kv.at[h], kv.at[h], cs.at[5], cr.at[3], (k, s, 1 - h)).start()
    third_stage(1)

    drain(sl.at[1 - h], cr.at[2])
    drain(kv.at[1 - h], cr.at[3])
    rows, wide = S * 2 * zi, 32 * zi
    m = lax.broadcasted_iota(jnp.int32, (rows, wide), 0)
    n = lax.broadcasted_iota(jnp.int32, (rows, wide), 1)
    q = m // zi
    place = (4 * (q // 2) + 2 * xh + q % 2) * 8 + 4 * h
    same = (m % zi) == (n % zi)
    spread = jnp.where(
        lax.broadcasted_iota(jnp.int32, (128, wide), 0) == lax.broadcasted_iota(jnp.int32, (128, wide), 1) // zi, 1.0, 0.0).astype(BF16)
    place = place.astype(F32)
    for half in range(2):
        slots = sl[half].astype(F32).reshape(wide, 128).astype(BF16)
        named = jnp.dot(kv[half].astype(BF16), spread, preferred_element_type=F32)
        where = jnp.broadcast_to(named[0:1, :], (rows, wide))
        for jj in range(4):
            pick = jnp.where(same & (where == place + float(jj)), 1.0, 0.0).astype(BF16)
            ad[half, :, jj * 128:(jj + 1) * 128] = jnp.dot(pick, slots, preferred_element_type=F32).astype(BF16)

    driven(0)
    for b in range(4):
        ov[b * 128:(b + 1) * 128] = jnp.dot(iv[b], dr[0, b], preferred_element_type=F32).astype(BF16)
    newest = ov[...]
    for half in range(2):
        made = jnp.dot(ad[half], newest, preferred_element_type=F32).astype(BF16)
        for other in range(S):
            us[other * 2 + half] = made[other * 2 * zi:(other + 1) * 2 * zi]

    for d in list(range(S, 2 * S)) + list(range(1, S)):
        other = wrap(e + d, 2 * S)
        rcopy(us.at[other], ur.at[e], uss.at[0], urs.at[0], (k, lax.div(other, 2), lax.rem(other, 2))).start()

    rest = field(1)
    drain(ur.at[pl.ds(0, 2 * S - 1)], urs.at[0])
    ur[e] = us[e]
    gather(1, rest + jnp.sum(ur[...].astype(F32), axis=0))
    for step in range(2):
        for d in range(3):
            drain(pa.at[step, 0], a1s.at[step, d])
            drain(qb.at[step, 0], b2s.at[step, d])
        for d in range(Y - 1):
            drain(pb.at[step, 0], b1s.at[step, d])
            drain(qa.at[step, 0], a2s.at[step, d])
        drain(zs.at[step, pl.ds(0, Z - 1)], zss.at[step])
    drain(us.at[pl.ds(0, 2 * S - 1)], uss.at[0])

    @pl.when(k < K - 1)
    def _():
        drain(x1.at[mine], hs.at[0])

    @pl.when(k > 0)
    def _():
        drain(x1.at[mine], hs.at[1])

    @pl.when(k == 0)
    def _():
        drain(bv.at[pl.ds(0, 32 - 32 // Z)], cs.at[0])
        drain(acc.at[0, pl.ds(0, 8 * (Z - 1))], cs.at[1])

    @pl.when(xh == 0)
    def _():
        drain(sl.at[h], cs.at[2])
        drain(kv.at[h], cs.at[3])

    drain(sl.at[h], cs.at[4])
    drain(kv.at[h], cs.at[5])
    drain(dv.at[0, pl.ds(0, K - 1)], gss.at[0])
    driven(1)
    drain(dv.at[1, pl.ds(0, K - 1)], gss.at[1])

    for step in range(2):
        pltpu.make_async_copy(dr.at[step], out.at[step], os.at[step]).wait()


def pin(array):
    return pltpu.with_memory_space_constraint(array, pltpu.HBM)


def shards(K, S, blocks, coords, counts, history, excitation, inverse):
    Y, Z = S // 2, K // 2
    zi = 128 // Z
    dma = pltpu.SemaphoreType.DMA
    v = pltpu.VMEM
    scratch = [
        v((2, 32), jnp.int32), v((8, 128), jnp.int32), pltpu.SMEM((8, 128), jnp.int32), v((8, 128), F32),
        v((32, 128, 128), BF16), v((Z, 32, zi, 128), BF16), v((8, 128, 128), BF16), v((8, 128, 128), BF16), v((2, 2, zi, 128), BF16), v((4, 128, 128), BF16),
        v((33, 128, 128), F32), v((2, 4, 128, 128), BF16),
        v((2, 4, Y, 128, 128), BF16), v((2, Y, 4, 128, 128), BF16),
        v((2, 3, Y, 128, 128), BF16), v((2, Y - 1, 4, 128, 128), BF16),
        v((2, Y, 128, 128), BF16), v((2, 4, 128, 128), BF16),
        v((2, Y - 1, 128, 128), BF16), v((2, 3, 128, 128), BF16),
        v((2, Z, 2 * zi, 128), BF16), v((2, Z, 2 * zi, 128), BF16), v((2, K, 2 * zi, 128), BF16),
        v((2, 32, zi, 128), BF16), v((2, 8, 128), F32), v((2, S * 2 * zi, 512), BF16),
        v((2 * S, 2 * zi, 128), BF16), v((2 * S, 2 * zi, 128), BF16), v((512, 128), BF16),
        dma((10,)), dma((2, 3)), dma((2, 3)), dma((2, Y - 1)), dma((2, Y - 1)),
        dma((2, Y - 1)), dma((2, Y - 1)), dma((2, 3)), dma((2, 3)),
        dma((2,)), dma((2,)), dma((2,)), dma((2,)), dma((1,)), dma((1,)), dma((2,)), dma((2,)), dma((6,)), dma((4,)), dma((2,)),
        pltpu.SemaphoreType.REGULAR((4,)),
    ]
    hbm = pl.BlockSpec(memory_space=pltpu.HBM)
    made = pl.pallas_call(
        functools.partial(kernel, K, Y),
        out_shape=jax.ShapeDtypeStruct((2, 4, 128, 128), BF16),
        in_specs=[hbm, pl.BlockSpec(memory_space=pltpu.SMEM)] + [hbm] * 4,
        out_specs=pl.BlockSpec(memory_space=pl.ANY),
        scratch_shapes=scratch,
        compiler_params=pltpu.CompilerParams(
            collective_id=0, has_side_effects=True, vmem_limit_bytes=40 * 1024 * 1024),
        name="march",
    )(
        pin(coords[0, 0, 0].T), counts[0, 0], pin(blocks[0, 0, 0]), pin(history[0].reshape(8, 128, 128)),
        pin(excitation[:, 0].reshape(2, 4, 128, 128)), pin(inverse[0]),
    )
    both = jnp.broadcast_to(inverse[0][None], made.shape)
    currents = jnp.einsum("nbij,nbjw->nbiw", both, made, preferred_element_type=F32)
    return currents.astype(BF16).reshape(2, 1, 512, 128)


def solution(mesh):
    placed = (
        P("delay", "src", "tgt", None, None, None),
        P("delay", "src", "tgt", None, None),
        P("delay", "src", "tgt"),
        P("delay", None, "src", None),
        P(None, "tgt", "src", None),
        P("tgt", "src", None, None),
    )
    return jax.shard_map(
        functools.partial(shards, mesh.shape["delay"], mesh.shape["src"]),
        mesh=mesh, in_specs=placed, out_specs=P(None, "tgt", "src", None), check_vma=False,
    )
```
